32 devices in a mesh: video: 2 (over y), block: 4 (over z), band: 2 (over x), chan: 2 (over core).
Axes of the slice: x: 2, y: 2, z: 4, core: 2. Of those that a mesh axis runs over, the one named last changes fastest.
Arguments:
- latents: bfloat16 [32, 2, 1664], P(('video', 'block'), 'band'), parts along dimension 0, may hold values from -60 to 60
- frame_counts: int32 [8], P('video'), parts along dimension 0, may hold values from 1 to 4, 8 in all
- w_in: bfloat16 [3, 3, 3, 16, 384], replicated, may hold values from -0.3125 to 0.3125
- gain_in: float32 [384], replicated, may hold values from 0.1 to 1.9
- shift_in: float32 [384], replicated, may hold values from -3 to 3
- w_mid: bfloat16 [3, 3, 3, 384, 384], P(None, None, None, None, 'chan'), may hold values from -0.0625 to 0.0625
- gain_out: float32 [384], P('chan'), may hold values from 0.1 to 1.9
- shift_out: float32 [384], P('chan'), may hold values from -3 to 3
Outputs:
- decoded: bfloat16 [32, 2, 104, 384], P(('video', 'block'), 'band', None, 'chan'), parts along dimension 0
The draws below stay inside these ranges and needn't reach their ends.
There are 2 independent parts, one for each index of `video`. The reference program is written for one: setup_inputs(seed, part) draws one part's arguments, and reference() takes and returns one part's arrays. A program takes and returns all parts, laid end to end along the dimension named above; an argument that names none is the same for every part. Nothing has to cross between parts.
Inputs may be any that keep to these rules, and one draw needn't show every extreme that they name: `frame_counts`: entry k is the number of consecutive latent frames that device k of the frame axis holds; the entries sum to 8.
All inputs are finite; a program needn't handle non-finite values.
Results may differ from the reference program's by a relative error of at most 0.013.
Values may be sent and summed in bfloat16 or wider, within the bound.
No kernel may reach another device: no remote copies, remote signals or barrier semaphores. Data moves between devices by JAX's collectives and lax.ppermute only.
A program may use at most 64 MiB of HBM per device.

```python
import math
import jax
import jax.numpy as jnp
import numpy as np
from jax import lax

LAT = 16
C = 384
GROUPS = 32
COLS = 104
AVG = 2
MOST = 4
ROWS = 2
FRAMES = 8
SLOTS = 16
N_BLOCK = 4


def draw_latents(key, part):
    first_key, second_key, third_key = jax.random.split(jax.random.fold_in(key, 17), 3)
    row_place = jnp.arange(ROWS, dtype=jnp.float32)
    row_scale = jnp.exp(jax.random.uniform(second_key, (ROWS,), jnp.float32) * math.log(10.0)) / math.sqrt(10.0)
    col_scale = jnp.exp(jax.random.uniform(third_key, (COLS,), jnp.float32) * math.log(10.0)) / math.sqrt(10.0)
    base_values = jnp.clip(jax.random.normal(first_key, (SLOTS, ROWS, COLS, LAT), jnp.float32), -3.0, 3.0)
    row_scale = row_scale * jnp.sqrt(1.0 + 2.0 * row_place)
    scaled = base_values * row_scale[None, :, None, None] * col_scale[None, None, :, None]
    return scaled.reshape(SLOTS, ROWS, COLS * LAT).astype(jnp.bfloat16)


def shard_levels(own_key, dims, cuts, least, high):
    factor_of = 1.0
    for axis_at, shards_of in cuts:
        draws = jax.random.uniform(jax.random.fold_in(jax.random.fold_in(own_key, 6), axis_at), (shards_of,), jnp.float32, least / len(cuts), high / len(cuts))
        factor_of = factor_of * jnp.repeat(jnp.exp(draws), dims[axis_at] // shards_of).reshape((-1,) + (1,) * (len(dims) - 1 - axis_at))
    return factor_of


def length_profile(count, total, reach, skew):
    weights = [(1 << 20) // math.isqrt(grade ** skew) + 1 for grade in range(2, count + 1)]
    surplus, counts = total - reach - (count - 1), [1] * (count - 1)
    while surplus > 0:
        candidates = [i for i in range(count - 1) if counts[i] < reach]
        whole, left = sum([weights[i] for i in candidates]), surplus
        for i in candidates:
            extra = min(reach - counts[i], max(1, left * weights[i] // whole), surplus)
            counts[i] = counts[i] + extra
            surplus = surplus - extra
    return np.array([reach] + counts)


def ragged(key, count, total, reach, skew):
    if count == 2:
        one = jax.random.randint(key, (), max(1, total - reach), min(reach, total - 1) + 1)
        return jnp.stack([one, total - one])
    lengths = jnp.asarray(length_profile(count, total, reach, skew), jnp.int32)
    pairs = (count - 1) // 2
    donor, receiver = lengths[1:1 + 2 * pairs:2], lengths[2:2 + 2 * pairs:2]
    room = jnp.minimum(donor - 1, reach - receiver)
    moved = jax.random.randint(jax.random.fold_in(key, 1), (pairs,), 0, 1 << 20) % (room + 1)
    lengths = lengths.at[1:1 + 2 * pairs:2].set(donor - moved).at[2:2 + 2 * pairs:2].set(receiver + moved)
    return lengths[jax.random.permutation(jax.random.fold_in(key, 2), count)]


def normal_values(rng, shape, scale, limit, shards=(), kind=jnp.bfloat16):
    array = scale * jax.random.normal(rng, shape, jnp.float32)
    if shards:
        array = array * shard_levels(rng, shape, shards, -0.22, 0.18)
    return jnp.clip(array, -limit, limit).astype(kind)


def setup_inputs(seed: int = 0, part: int = 0) -> dict:
    key_list = jax.random.split(jax.random.key(seed), 9)
    part_keys = jax.random.split(jax.random.fold_in(key_list[8], part), 9)
    return {
        "latents": draw_latents(jax.random.fold_in(jax.random.fold_in(key_list[8], part), 71), part),
        "frame_counts": ragged(part_keys[1], N_BLOCK, AVG * N_BLOCK, MOST, 2).astype(jnp.int32),
        "w_in": normal_values(key_list[2], (3, 3, 3, LAT, C), (27 * LAT) ** -0.5, 0.3125),
        "gain_in": jnp.clip(1.0 + 0.18 * jax.random.normal(key_list[3], (C,), jnp.float32), 0.1, 1.9),
        "shift_in": normal_values(key_list[4], (C,), 0.5, 3.0, (), jnp.float32),
        "w_mid": normal_values(key_list[5], (3, 3, 3, C, C), (27 * C) ** -0.5, 0.0625, ((4, 2),)),
        "gain_out": jnp.clip(1.0 + 0.18 * jax.random.normal(key_list[6], (C,), jnp.float32), 0.1, 1.9),
        "shift_out": normal_values(key_list[7], (C,), 0.5, 3.0, ((0, 2),), jnp.float32),
    }


EPSILON = 1e-06

def causal_conv(inputs, kernel):
    count_in, rows_in, cols_in, width_in = inputs.shape
    out_width = kernel.shape[4]
    padded = jnp.pad(inputs, ((2, 0), (1, 1), (1, 1), (0, 0)))
    accumulate = jnp.zeros((count_in * rows_in * cols_in, out_width), jnp.float32)
    for step_t in range(3):
        for step_y in range(3):
            patches = [padded[step_t:step_t + count_in, step_y:step_y + rows_in, step_x:step_x + cols_in, :] for step_x in range(3)]
            stacked = jnp.concatenate(patches, axis=-1).reshape(-1, 3 * width_in)
            accumulate = accumulate + jnp.dot(stacked, kernel[step_t, step_y].reshape(3 * width_in, out_width), preferred_element_type=jnp.float32)
    return accumulate.reshape(count_in, rows_in, cols_in, out_width)

def group_silu(values, norm_gain, norm_shift):
    count_in = values.shape[0]
    group_width = C // GROUPS
    grouped = values.reshape(count_in, ROWS * COLS, GROUPS, group_width)
    group_total = lax.optimization_barrier(jnp.sum(grouped, axis=(1, 3)))
    squares = lax.optimization_barrier(jnp.sum(grouped * grouped, axis=(1, 3)))
    total = float(ROWS * COLS * group_width)
    group_mean = group_total / total
    variance = squares / total - group_mean * group_mean
    inverse = lax.rsqrt(variance + EPSILON)
    normed = (grouped - group_mean[:, None, :, None]) * inverse[:, None, :, None]
    normed = normed.reshape(values.shape)
    return jax.nn.silu(normed * norm_gain + norm_shift)

def reference(latents, frame_counts, w_in, gain_in, shift_in, w_mid, gain_out, shift_out):
    run_ends = jnp.cumsum(frame_counts).astype(jnp.int32)
    run_starts = (run_ends - frame_counts).astype(jnp.int32)
    frame_ids = jnp.arange(FRAMES, dtype=jnp.int32)
    owners = lax.optimization_barrier(jnp.sum((frame_ids[:, None] >= run_ends[None, :]).astype(jnp.int32), axis=1)).astype(jnp.int32)
    slot_ids = (owners * MOST + frame_ids - jnp.take(run_starts, owners)).astype(jnp.int32)
    video_frames = jnp.take(latents, slot_ids, axis=0).reshape(FRAMES, ROWS, COLS, LAT)
    first_conv = causal_conv(video_frames, w_in).astype(jnp.bfloat16)
    activated = group_silu(first_conv.astype(jnp.float32), gain_in, shift_in).astype(jnp.bfloat16)
    second_conv = causal_conv(activated, w_mid).astype(jnp.bfloat16)
    second_norm = group_silu(second_conv.astype(jnp.float32), gain_out, shift_out).astype(jnp.bfloat16)
    all_slots = jnp.arange(SLOTS, dtype=jnp.int32)
    devices_of = (all_slots // MOST).astype(jnp.int32)
    places = (all_slots % MOST).astype(jnp.int32)
    alive_mask = places < jnp.take(frame_counts, devices_of)
    sources = jnp.clip(jnp.take(run_starts, devices_of) + places, 0, FRAMES - 1).astype(jnp.int32)
    picked = jnp.take(second_norm, sources, axis=0)
    return jnp.where(alive_mask[:, None, None, None], picked, jnp.zeros_like(picked))
```

```python
import functools

import jax
import jax.numpy as jnp
from jax import lax
from jax.experimental import pallas as pl
from jax.experimental.pallas import tpu as pltpu
from jax.sharding import PartitionSpec as P

LAT = 16
C = 384
GROUPS = 32
WIDTH = C // GROUPS
EPSILON = 1e-06
LANES = 128
COLS_IN_TILE = LANES // LAT


def ring_place(chip_block, chip_band, blocks):
    return jnp.where(chip_band == 0, chip_block, 2 * blocks - 1 - chip_block)


def ring_moves(blocks, shift_first, shift_second):
    ring = [(b, 0) for b in range(blocks)] + [(b, 1) for b in reversed(range(blocks))]
    count = len(ring)
    moves = []
    for core, shift in ((0, shift_first), (1, shift_second)):
        for place in range(count):
            b, a = ring[place]
            b2, a2 = ring[(place + shift) % count]
            moves.append(((b * 2 + a) * 2 + core, (b2 * 2 + a2) * 2 + core))
    return moves


def pack_body(*refs):
    out = refs[-1]
    for i, ref in enumerate(refs[:-1]):
        out[i] = ref[0]


def pack(*parts):
    vmem = pl.BlockSpec(memory_space=pltpu.VMEM)
    return pl.pallas_call(
        pack_body,
        out_shape=jax.ShapeDtypeStruct((len(parts),) + parts[0].shape[1:], parts[0].dtype),
        in_specs=[vmem] * len(parts),
        out_specs=vmem,
        compiler_params=pltpu.CompilerParams(vmem_limit_bytes=1024 * 1024),
    )(*parts)


def exchange_ring(latents, kept):
    axes = ("block", "band", "chan")
    blocks = lax.axis_size("block")
    swap = [(2 * n + c, 2 * n + 1 - c) for n in range(2 * blocks) for c in range(2)]
    own = latents
    first = lax.ppermute(own, axes, ring_moves(blocks, 1, 2))
    second = lax.ppermute(first, axes, swap)
    held = pack(kept, first, second)
    third = lax.ppermute(held, axes, ring_moves(blocks, 3, 6))
    fourth = lax.ppermute(third, axes, swap)
    return [kept, first, second, third, fourth]


def piece_ring(block, band, owner, row, blocks):
    core = lax.axis_index("chan")
    count = 2 * blocks
    mine = ring_place(block, band, blocks)
    other = ring_place(owner, row, blocks)
    back = lax.rem(mine - other + count, count)
    base = jnp.where(back >= 6, 2, jnp.where(back >= 3, 1, 0))
    rest = back - 3 * base
    group = jnp.where(base == 0, 0, jnp.where(core == 0, base, 3 - base))
    order = jnp.where(base == 0, core, base - 1)
    place = jnp.where((order == 0) | (rest == 0), rest, 3 - rest)
    return group * 3 + place


def group_matrix(width):
    rows = lax.broadcasted_iota(jnp.int32, (width, width), 0)
    cols = lax.broadcasted_iota(jnp.int32, (width, width), 1)
    low = cols - lax.rem(cols, WIDTH)
    same = (rows >= low) & (rows < low + WIDTH)
    return jnp.where(same, 1.0, 0.0).astype(jnp.bfloat16)


def group_sums(sums, matrix):
    high = sums.astype(jnp.bfloat16)
    rest = sums - high.astype(jnp.float32)
    middle = rest.astype(jnp.bfloat16)
    low = (rest - middle.astype(jnp.float32)).astype(jnp.bfloat16)
    rows = sums.shape[0]
    parts = jnp.concatenate([high, middle, low], axis=0)
    out = jnp.dot(parts, matrix, preferred_element_type=jnp.float32)
    return out[:rows] + out[rows : 2 * rows] + out[2 * rows :]


def silu(u):
    return u / (1.0 + jnp.exp(-u))


def prepare_body(rows, *refs):
    latents, w_in, gain_in, shift_in, w_mid, gain_out, shift_out = refs[:7]
    own, wide, matrix, kernel, flat_terms, tall_terms = refs[7:13]
    small, flat_parts, tall_parts, sems = refs[13:]
    half = tall_terms.shape[1]
    depth = wide.shape[0] // 3
    pairs = (
        (latents, own),
        (w_in, small),
        (gain_in, flat_parts.at[0]),
        (shift_in, flat_parts.at[1]),
        (gain_out, tall_parts.at[0]),
        (shift_out, tall_parts.at[1]),
        (w_mid, kernel),
    )
    loads = [pltpu.make_async_copy(a, b, sems.at[i]) for i, (a, b) in enumerate(pairs)]
    for load in loads:
        load.start()
    wide[...] = jnp.zeros_like(wide)
    matrix[...] = group_matrix(C)
    eye = lax.broadcasted_iota(jnp.int32, (half, half), 0) == lax.broadcasted_iota(
        jnp.int32, (half, half), 1
    )
    for load in loads[:-1]:
        load.wait()
    for t in range(3):
        for place in range(rows):
            for r in range(rows):
                y = place - r + 1
                if 0 <= y <= 2:
                    top = t * depth + place * 64
                    wide[top : top + 3 * LAT, r * C : (r + 1) * C] = small[t, y]
    for i in range(2):
        flat_terms[i : i + 1] = flat_parts[i].reshape(1, C)
        spread = jnp.where(eye, tall_parts[i].reshape(1, half), 0.0)
        tall_terms[i] = jnp.broadcast_to(jnp.sum(spread, axis=1, keepdims=True), (half, LANES))
    loads[-1].wait()


def prepare(rows, own, w_in, gain_in, shift_in, w_mid, gain_out, shift_out):
    half = w_mid.shape[4]
    pairs = -(-rows // 2)
    small = (3, 3, 3 * LAT, C)
    operands = (
        own,
        w_in.reshape(small),
        gain_in,
        shift_in,
        jnp.transpose(w_mid, (0, 1, 2, 4, 3)).reshape(3, 3, 3 * half, C),
        gain_out,
        shift_out,
    )
    return pl.pallas_call(
        functools.partial(prepare_body, rows),
        out_shape=(
            pltpu.VMEM(own.shape, own.dtype),
            pltpu.VMEM((3 * pairs * LANES, rows * C), jnp.bfloat16),
            pltpu.VMEM((C, C), jnp.bfloat16),
            pltpu.VMEM((3, 3, 3 * half, C), jnp.bfloat16),
            pltpu.VMEM((8, C), jnp.float32),
            pltpu.VMEM((2, half, LANES), jnp.float32),
        ),
        in_specs=[pl.BlockSpec(memory_space=pltpu.HBM)] * 7,
        out_specs=(pl.BlockSpec(memory_space=pltpu.VMEM),) * 6,
        scratch_shapes=[
            pltpu.VMEM(small, jnp.bfloat16),
            pltpu.VMEM((2, C), jnp.float32),
            pltpu.VMEM((2, half), jnp.float32),
            pltpu.SemaphoreType.DMA((7,)),
        ],
        compiler_params=pltpu.CompilerParams(vmem_limit_bytes=16 * 1024 * 1024),
    )(*[pltpu.with_memory_space_constraint(a, pltpu.HBM) for a in operands])


def body(cfg, *refs):
    blocks, rows, frames, columns, pieces, use_ring = cfg
    n_arrays = len(pieces)
    sources = refs[:n_arrays]
    (counts_in, wide, matrix, kernel, flat_terms, tall_terms, out) = refs[n_arrays : n_arrays + 7]
    (counts, slabs, patches, first, acts, second, sem) = refs[n_arrays + 7 :]
    half = out.shape[2]
    chunks = columns // COLS_IN_TILE
    slab = -(-(chunks + 1) // 8) * 8
    padded = -(-(columns + 1) // 16) * 16
    stride = -(-(columns + 1) // LANES) * LANES
    halo = 4
    lat_frames = frames + halo
    act_frames = frames + 2
    pairs = -(-rows // 2)
    depth = pairs * LANES
    own_rows = out.shape[1]
    block = lax.axis_index("block")
    band = lax.axis_index("band")

    load = pltpu.make_async_copy(counts_in, counts, sem)
    load.start()

    slabs[...] = jnp.zeros_like(slabs)
    at = 0
    for source, n in zip(sources, pieces):
        for p in range(n):
            values = source[p].astype(jnp.float32)
            for b in range(chunks):
                slabs[pl.ds(at * frames * slab + b, frames, stride=slab), :] = values[
                    :, b * LANES : (b + 1) * LANES
                ]
            at += 1

    load.wait()
    my_start = jnp.int32(0)
    for k in range(blocks):
        my_start = my_start + jnp.where(k < block, counts[k], 0)
    my_count = counts[block]

    lane = lax.broadcasted_iota(jnp.int32, (slab, LANES), 1)
    patches[...] = jnp.zeros_like(patches)
    for f in range(lat_frames):
        if f < halo:
            wanted = my_start - halo + f
            valid = wanted >= 0
            safe = jnp.maximum(wanted, 0)
            total, begin, owner = jnp.int32(0), jnp.int32(0), jnp.int32(0)
            for k in range(blocks):
                total = total + counts[k]
                past = safe >= total
                owner = owner + jnp.where(past, 1, 0)
                begin = jnp.where(past, total, begin)
            slot = safe - begin
        else:
            valid, owner, slot = None, block, jnp.int32(f - halo)
        planes = []
        for r in range(rows):
            rank, inner = r // own_rows, r % own_rows
            if use_ring:
                piece = piece_ring(block, band, owner, rank, blocks)
            else:
                piece = owner * (rows // own_rows) + rank
            piece = piece * own_rows + inner
            top = pl.multiple_of((piece * frames + slot) * slab, 8)
            plane = slabs[pl.ds(top, slab), :]
            if valid is not None:
                plane = jnp.where(valid, plane, 0.0)
            planes.append(plane)
        if rows % 2:
            planes.append(jnp.zeros_like(planes[0]))
        for g in range(pairs):
            left, right = planes[2 * g], pltpu.roll(planes[2 * g + 1], 64, 1)
            for j in range(COLS_IN_TILE):
                begin_lane = LAT * (j - 1)
                a, b = left, right
                if j == 0:
                    a = jnp.where(lane >= LANES - LAT, pltpu.roll(left, 1, 0), left)
                    b = jnp.where(
                        (lane >= 64 - LAT) & (lane < 64), pltpu.roll(right, 1, 0), right
                    )
                if j == COLS_IN_TILE - 1:
                    a = jnp.where(lane < LAT, pltpu.roll(left, slab - 1, 0), left)
                    b = jnp.where(
                        (lane >= 64) & (lane < 64 + LAT), pltpu.roll(right, slab - 1, 0), right
                    )
                low = begin_lane % LANES
                if low + 64 <= LANES:
                    inside = (lane >= low) & (lane < low + 64)
                else:
                    inside = (lane >= low) | (lane < low + 64 - LANES)
                mixed = pltpu.roll(jnp.where(inside, a, b), (-begin_lane) % LANES, 1)
                patches[
                    pl.ds((g * lat_frames + f) * padded + j, chunks, stride=COLS_IN_TILE), :
                ] = mixed[:chunks]

    low_patches = patches[...].astype(jnp.bfloat16)
    stacked = jnp.concatenate(
        [
            low_patches[(g * lat_frames + t) * padded : (g * lat_frames + t + act_frames) * padded]
            for t in range(3)
            for g in range(pairs)
        ],
        axis=1,
    )
    first[...] = jnp.dot(stacked, wide[...], preferred_element_type=jnp.float32)

    sums, squares = [], []
    for g in range(act_frames):
        plain = jnp.zeros((1, C), jnp.float32)
        square = jnp.zeros((1, C), jnp.float32)
        for r in range(rows):
            part = first[g * padded : (g + 1) * padded, r * C : (r + 1) * C]
            plain = plain + jnp.sum(part, axis=0, keepdims=True)
            square = square + jnp.sum(part * part, axis=0, keepdims=True)
        sums.append(plain)
        squares.append(square)
    fill = [jnp.zeros((1, C), jnp.float32)] * (-(2 * act_frames) % 16)
    totals = group_sums(jnp.concatenate(sums + squares + fill, axis=0), matrix[...])
    size = float(rows * columns * WIDTH)
    mean = totals[:act_frames] / size
    variance = totals[act_frames : 2 * act_frames] / size - mean * mean
    scale = lax.rsqrt(variance + EPSILON) * flat_terms[0:1]
    shift = flat_terms[1:2] - mean * scale
    for g in range(act_frames):
        live = my_start - 2 + g >= 0
        scale_g = jnp.where(live, scale[g : g + 1], 0.0)
        shift_g = jnp.where(live, shift[g : g + 1], 0.0)
        for r in range(rows):
            part = first[g * padded : g * padded + columns, r * C : (r + 1) * C]
            act = silu(part * scale_g + shift_g)
            act = jnp.concatenate([act, jnp.zeros((stride - columns, C), jnp.float32)], axis=0)
            acts[g * stride : (g + 1) * stride, r * C : (r + 1) * C] = act.astype(jnp.bfloat16)

    span = frames * stride
    inside = lax.broadcasted_iota(jnp.int32, (half, stride), 1) < columns
    spans = {}
    for r in range(rows):
        spans.setdefault((max(0, r - 1), min(rows - 1, r + 1)), []).append(r)
    for (low, high), members in spans.items():
        places = range(low, high + 1)
        positions = jnp.concatenate(
            [
                acts[t * stride : t * stride + span, place * C : (place + 1) * C]
                for place in places
                for t in range(3)
            ],
            axis=1,
        )
        weights = jnp.concatenate(
            [
                jnp.concatenate(
                    [kernel[t, place - r + 1] for place in places for t in range(3)], axis=1
                )
                for r in members
            ],
            axis=0,
        )
        taps = lax.dot_general(
            weights, positions, (((1,), (1,)), ((), ())), preferred_element_type=jnp.float32
        )
        for m, r in enumerate(members):
            top = m * 3 * half
            for f in range(frames):
                left = f * stride
                tap = [
                    taps[top + s * half : top + (s + 1) * half, left : left + stride]
                    for s in range(3)
                ]
                value = tap[1] + pltpu.roll(tap[0], 1, 1) + pltpu.roll(tap[2], stride - 1, 1)
                second[r, f] = jnp.where(inside, value, 0.0)

    lane_at = lax.broadcasted_iota(jnp.int32, (half, LANES), 1)
    columns_of = jnp.zeros((half, LANES), jnp.float32)
    for f in range(frames):
        plain, square = second[0, f], second[0, f] * second[0, f]
        for r in range(1, rows):
            plain = plain + second[r, f]
            square = square + second[r, f] * second[r, f]
        columns_of = jnp.where(lane_at == f, jnp.sum(plain, axis=1, keepdims=True), columns_of)
        columns_of = jnp.where(
            lane_at == frames + f, jnp.sum(square, axis=1, keepdims=True), columns_of
        )
    high = columns_of.astype(jnp.bfloat16)
    rest = columns_of - high.astype(jnp.float32)
    middle = rest.astype(jnp.bfloat16)
    low = (rest - middle.astype(jnp.float32)).astype(jnp.bfloat16)
    matrix2 = matrix[:half, :half]
    totals = (
        jnp.dot(matrix2, high, preferred_element_type=jnp.float32)
        + jnp.dot(matrix2, middle, preferred_element_type=jnp.float32)
        + jnp.dot(matrix2, low, preferred_element_type=jnp.float32)
    )
    mean = totals / size
    variance = pltpu.roll(mean, LANES - frames, 1) - mean * mean
    scale = lax.rsqrt(variance + EPSILON) * tall_terms[0]
    shift = tall_terms[1] - mean * scale
    for f in range(frames):
        for inner in range(own_rows):
            part = second[band * own_rows + inner, f]
            value = silu(part * scale[:, f : f + 1] + shift[:, f : f + 1])
            value = jnp.where(f < my_count, value, 0.0).astype(out.dtype)
            out[f, inner] = value[:, :columns]


def shards(latents, frame_counts, w_in, gain_in, shift_in, w_mid, gain_out, shift_out):
    frames, own_rows, flat = latents.shape
    columns = flat // LAT
    half = w_mid.shape[4]
    blocks, bands = lax.axis_size("block"), lax.axis_size("band")
    rows = own_rows * bands
    use_ring = blocks == 4 and bands == 2 and own_rows == 1 and lax.axis_size("chan") == 2
    own = jnp.transpose(latents, (1, 0, 2))
    kept, *prepared = prepare(rows, own, w_in, gain_in, shift_in, w_mid, gain_out, shift_out)
    if use_ring:
        sources = exchange_ring(own, kept)
    else:
        gathered = lax.all_gather(own, ("block", "band"), axis=0)
        sources = [gathered.reshape(-1, frames, flat)]
    pieces = tuple(a.shape[0] for a in sources)
    chunks = columns // COLS_IN_TILE
    slab = -(-(chunks + 1) // 8) * 8
    padded = -(-(columns + 1) // 16) * 16
    stride = -(-(columns + 1) // LANES) * LANES
    pairs = -(-rows // 2)
    cfg = (blocks, rows, frames, columns, pieces, use_ring)
    vmem = pl.BlockSpec(memory_space=pltpu.VMEM)
    decoded = pl.pallas_call(
        functools.partial(body, cfg),
        out_shape=jax.ShapeDtypeStruct((frames, own_rows, half, columns), jnp.bfloat16),
        in_specs=[vmem] * len(sources)
        + [pl.BlockSpec(memory_space=pltpu.HBM)]
        + [vmem] * 5,
        out_specs=vmem,
        scratch_shapes=[
            pltpu.SMEM((blocks,), jnp.int32),
            pltpu.VMEM((sum(pieces) * frames * slab, LANES), jnp.float32),
            pltpu.VMEM((pairs * (frames + 4) * padded, LANES), jnp.float32),
            pltpu.VMEM(((frames + 2) * padded, rows * C), jnp.float32),
            pltpu.VMEM(((frames + 2) * stride, rows * C), jnp.bfloat16),
            pltpu.VMEM((rows, frames, half, stride), jnp.float32),
            pltpu.SemaphoreType.DMA,
        ],
        compiler_params=pltpu.CompilerParams(vmem_limit_bytes=32 * 1024 * 1024),
    )(*sources, pltpu.with_memory_space_constraint(frame_counts, pltpu.HBM), *prepared)
    return jnp.transpose(decoded, (0, 1, 3, 2))


def solution(mesh):
    return jax.shard_map(
        shards,
        mesh=mesh,
        in_specs=(
            P(("video", "block"), "band", None),
            P("video"),
            P(),
            P(),
            P(),
            P(None, None, None, None, "chan"),
            P("chan"),
            P("chan"),
        ),
        out_specs=P(("video", "block"), "band", None, "chan"),
        check_vma=False,
    )
```

```python
import functools

import jax
import jax.numpy as jnp
from jax import lax
from jax.experimental import pallas as pl
from jax.experimental.pallas import tpu as pltpu
from jax.sharding import PartitionSpec as P


LAT = 16
C = 384
GROUPS = 32
WIDTH = C // GROUPS
EPSILON = 1e-06
LANES = 128
COLS_IN_TILE = LANES // LAT


FIRST_ROUND = (
    ((0, 1), (2, 0), (1, 0), (3, 1)),
    ((1, 1), (3, 0), (0, 0), (2, 0)),
)
SECOND_ROUND = (
    ((1, 0), (0, 0), (3, 1), (2, 0)),
    ((1, 0), (3, 0), (0, 0), (2, 1)),
)


def round_moves(sources):
    moves = []
    for core in range(2):
        for block in range(4):
            for band in range(2):
                from_block, turn = sources[core][block]
                source = (from_block * 2 + (band ^ turn)) * 2 + core
                moves.append((source, (block * 2 + band) * 2 + core))
    return moves


def held_pieces(core, block):
    return [(block, 0), FIRST_ROUND[core][block], FIRST_ROUND[1 - core][block]]


def all_pieces(core, block):
    pieces = held_pieces(core, block)
    for who in (core, 1 - core):
        from_block, turn = SECOND_ROUND[who][block]
        pieces += [(b, t ^ turn) for b, t in held_pieces(who, from_block)]
    return pieces


def choose(index, values):
    out = jnp.int32(values[0])
    for i, value in enumerate(values[1:], 1):
        out = jnp.where(index == i, value, out)
    return out


def piece_finder(bands, use_ring):
    block, band = lax.axis_index("block"), lax.axis_index("band")
    if not use_ring:
        return lambda owner, rank: owner * bands + rank
    mine = lax.axis_index("chan") * 4 + block
    places = []
    for owner in range(4):
        for turn in range(2):
            column = []
            for core in range(2):
                for at in range(4):
                    found = all_pieces(core, at)
                    column.append(found.index((owner, turn)) if (owner, turn) in found else 0)
            places.append(choose(mine, column))
    return lambda owner, rank: choose(owner * 2 + lax.rem(rank + band, 2), places)


def pack_body(*refs):
    out = refs[-1]
    for i, ref in enumerate(refs[:-1]):
        out[i] = ref[0]


def pack(*parts):
    vmem = pl.BlockSpec(memory_space=pltpu.VMEM)
    return pl.pallas_call(
        pack_body,
        out_shape=jax.ShapeDtypeStruct((len(parts),) + parts[0].shape[1:], parts[0].dtype),
        in_specs=[vmem] * len(parts),
        out_specs=vmem,
        compiler_params=pltpu.CompilerParams(vmem_limit_bytes=1024 * 1024),
    )(*parts)


def exchange_ring(latents, kept):
    axes = ("block", "band", "chan")
    swap = [(2 * n + c, 2 * n + 1 - c) for n in range(8) for c in range(2)]
    first = lax.ppermute(latents, axes, round_moves(FIRST_ROUND))
    second = lax.ppermute(first, axes, swap)
    held = pack(kept, first, second)
    third = lax.ppermute(held, axes, round_moves(SECOND_ROUND))
    fourth = lax.ppermute(third, axes, swap)
    return [kept, first, second, third, fourth]


def group_matrix(width):
    rows = lax.broadcasted_iota(jnp.int32, (width, width), 0)
    cols = lax.broadcasted_iota(jnp.int32, (width, width), 1)
    low = cols - lax.rem(cols, WIDTH)
    same = (rows >= low) & (rows < low + WIDTH)
    return jnp.where(same, 1.0, 0.0).astype(jnp.bfloat16)


def group_sums(sums, matrix):
    high = sums.astype(jnp.bfloat16)
    rest = sums - high.astype(jnp.float32)
    middle = rest.astype(jnp.bfloat16)
    low = (rest - middle.astype(jnp.float32)).astype(jnp.bfloat16)
    rows = sums.shape[0]
    parts = jnp.concatenate([high, middle, low], axis=0)
    out = jnp.dot(parts, matrix, preferred_element_type=jnp.float32)
    return out[:rows] + out[rows : 2 * rows] + out[2 * rows :]


def silu(u):
    half_u = 0.5 * u
    return half_u + half_u * jnp.tanh(half_u)


HALO = 4


def prepare_body(cfg, *refs):
    blocks, rows, own_rows, frames, use_ring = cfg
    latents, w_in, gain_in, shift_in, gain_out, shift_out, counts_in, w_mid = refs[:8]
    own, wide, matrix, flat_terms, tall_terms, table, kernel = refs[8:15]
    small, flat_parts, tall_parts, counts, sems = refs[15:]
    half = tall_terms.shape[1]
    depth = wide.shape[0] // 3
    copies = (
        (counts_in, counts),
        (latents, own),
        (w_in, small),
        (gain_in, flat_parts.at[0]),
        (shift_in, flat_parts.at[1]),
        (gain_out, tall_parts.at[0]),
        (shift_out, tall_parts.at[1]),
        (w_mid.at[: kernel.shape[0]], kernel),
    )
    loads = [pltpu.make_async_copy(a, b, sems.at[i]) for i, (a, b) in enumerate(copies)]
    for load in loads:
        load.start()
    wide[...] = jnp.zeros_like(wide)
    matrix[...] = group_matrix(C)
    eye = lax.broadcasted_iota(jnp.int32, (half, half), 0) == lax.broadcasted_iota(
        jnp.int32, (half, half), 1
    )
    block = lax.axis_index("block")
    find = piece_finder(rows // own_rows, use_ring)
    loads[0].wait()
    my_start = jnp.int32(0)
    for k in range(blocks):
        my_start = my_start + jnp.where(k < block, counts[k], 0)
    entries = []
    for f in range(HALO):
        wanted = my_start - HALO + f
        safe = jnp.maximum(wanted, 0)
        total, begin, owner = jnp.int32(0), jnp.int32(0), jnp.int32(0)
        for k in range(blocks):
            total = total + counts[k]
            past = safe >= total
            owner = owner + jnp.where(past, 1, 0)
            begin = jnp.where(past, total, begin)
        for r in range(rows):
            piece = find(owner, r // own_rows) * own_rows + r % own_rows
            entries.append(jnp.where(wanted >= 0, piece * frames + safe - begin, -1))
    for r in range(rows):
        piece = find(block, r // own_rows) * own_rows + r % own_rows
        entries.append(piece * frames)
    entries += [my_start, counts[block]]
    lane = lax.broadcasted_iota(jnp.int32, table.shape, 1)
    line = jnp.zeros(table.shape, jnp.int32)
    for i, entry in enumerate(entries):
        line = jnp.where(lane == i, entry, line)
    table[...] = line
    for load in loads[1:-1]:
        load.wait()
    for t in range(3):
        for place in range(rows):
            for r in range(rows):
                y = place - r + 1
                if 0 <= y <= 2:
                    top = t * depth + place * 64
                    wide[top : top + 3 * LAT, r * C : (r + 1) * C] = small[t, y]
    for i in range(2):
        flat_terms[i : i + 1] = flat_parts[i].reshape(1, C)
        spread = jnp.where(eye, tall_parts[i].reshape(1, half), 0.0)
        tall_terms[i] = jnp.broadcast_to(jnp.sum(spread, axis=1, keepdims=True), (half, LANES))
    loads[-1].wait()


def in_hbm(a):
    return pltpu.with_memory_space_constraint(a, pltpu.HBM)


def prepare(cfg, own, w_in, gain_in, shift_in, gain_out, shift_out, counts, middle):
    blocks, rows = cfg[:2]
    half = gain_out.shape[0]
    pairs = -(-rows // 2)
    small = (3, 3, 3 * LAT, C)
    operands = (
        own,
        w_in.reshape(small),
        gain_in,
        shift_in,
        gain_out,
        shift_out,
        counts,
        middle,
    )
    return pl.pallas_call(
        functools.partial(prepare_body, cfg),
        out_shape=(
            pltpu.VMEM(own.shape, own.dtype),
            pltpu.VMEM((3 * pairs * LANES, rows * C), jnp.bfloat16),
            pltpu.VMEM((C, C), jnp.bfloat16),
            pltpu.VMEM((8, C), jnp.float32),
            pltpu.VMEM((2, half, LANES), jnp.float32),
            pltpu.VMEM((8, LANES), jnp.int32),
            pltpu.VMEM((1,) + middle.shape[1:], middle.dtype),
        ),
        in_specs=[pl.BlockSpec(memory_space=pltpu.HBM)] * 8,
        out_specs=(pl.BlockSpec(memory_space=pltpu.VMEM),) * 7,
        scratch_shapes=[
            pltpu.VMEM(small, jnp.bfloat16),
            pltpu.VMEM((2, C), jnp.float32),
            pltpu.VMEM((2, half), jnp.float32),
            pltpu.SMEM((blocks,), jnp.int32),
            pltpu.SemaphoreType.DMA((8,)),
        ],
        compiler_params=pltpu.CompilerParams(vmem_limit_bytes=16 * 1024 * 1024),
    )(*[in_hbm(a) for a in operands])


def load_body(w_mid, kernel, sem):
    count = kernel.shape[0]
    load = pltpu.make_async_copy(w_mid.at[3 - count :], kernel, sem)
    load.start()
    load.wait()


def load_rest(middle):
    return pl.pallas_call(
        load_body,
        out_shape=pltpu.VMEM((2,) + middle.shape[1:], middle.dtype),
        in_specs=[pl.BlockSpec(memory_space=pltpu.HBM)],
        out_specs=pl.BlockSpec(memory_space=pltpu.VMEM),
        scratch_shapes=[pltpu.SemaphoreType.DMA],
        compiler_params=pltpu.CompilerParams(vmem_limit_bytes=1024 * 1024),
    )(in_hbm(middle))


def body(cfg, *refs):
    rows, frames, columns, pieces = cfg
    n_arrays = len(pieces)
    sources = refs[:n_arrays]
    wide, matrix, flat_terms, tall_terms, table_in, kernel_0, kernel_1, out = refs[
        n_arrays : n_arrays + 8
    ]
    table, slabs, patches, first, acts, second, sem = refs[n_arrays + 8 :]
    half = out.shape[2]
    chunks = columns // COLS_IN_TILE
    slab = -(-(chunks + 1) // 8) * 8
    padded = -(-(columns + 1) // 16) * 16
    stride = -(-(columns + 1) // LANES) * LANES
    lat_frames = frames + HALO
    act_frames = frames + 2
    pairs = -(-rows // 2)
    own_rows = out.shape[1]
    load = pltpu.make_async_copy(table_in, table, sem)
    load.start()

    slabs[...] = jnp.zeros_like(slabs)
    at = 0
    for source, n in zip(sources, pieces):
        for p in range(n):
            values = source[p].astype(jnp.float32)
            for b in range(chunks):
                slabs[pl.ds(at * frames * slab + b, frames, stride=slab), :] = values[
                    :, b * LANES : (b + 1) * LANES
                ]
            at += 1

    load.wait()
    my_start = table[0, (HALO + 1) * rows]
    my_count = table[0, (HALO + 1) * rows + 1]
    lane = lax.broadcasted_iota(jnp.int32, (slab, LANES), 1)
    patches[...] = jnp.zeros_like(patches)
    for f in range(lat_frames):
        planes = []
        for r in range(rows):
            if f < HALO:
                at = table[0, f * rows + r]
                top = pl.multiple_of(jnp.maximum(at, 0) * slab, 8)
                planes.append(jnp.where(at >= 0, slabs[pl.ds(top, slab), :], 0.0))
            else:
                at = table[0, HALO * rows + r] + (f - HALO)
                planes.append(slabs[pl.ds(pl.multiple_of(at * slab, 8), slab), :])
        if rows % 2:
            planes.append(jnp.zeros_like(planes[0]))
        for g in range(pairs):
            left, right = planes[2 * g], pltpu.roll(planes[2 * g + 1], 64, 1)
            for j in range(COLS_IN_TILE):
                begin_lane = LAT * (j - 1)
                a, b = left, right
                if j == 0:
                    a = jnp.where(lane >= LANES - LAT, pltpu.roll(left, 1, 0), left)
                    b = jnp.where(
                        (lane >= 64 - LAT) & (lane < 64), pltpu.roll(right, 1, 0), right
                    )
                if j == COLS_IN_TILE - 1:
                    a = jnp.where(lane < LAT, pltpu.roll(left, slab - 1, 0), left)
                    b = jnp.where(
                        (lane >= 64) & (lane < 64 + LAT), pltpu.roll(right, slab - 1, 0), right
                    )
                low = begin_lane % LANES
                if low + 64 <= LANES:
                    inside = (lane >= low) & (lane < low + 64)
                else:
                    inside = (lane >= low) | (lane < low + 64 - LANES)
                mixed = pltpu.roll(jnp.where(inside, a, b), (-begin_lane) % LANES, 1)
                patches[
                    pl.ds((g * lat_frames + f) * padded + j, chunks, stride=COLS_IN_TILE), :
                ] = mixed[:chunks]

    low_patches = patches[...].astype(jnp.bfloat16)
    stacked = jnp.concatenate(
        [
            low_patches[(g * lat_frames + t) * padded : (g * lat_frames + t + act_frames) * padded]
            for t in range(3)
            for g in range(pairs)
        ],
        axis=1,
    )
    first[...] = jnp.dot(stacked, wide[...], preferred_element_type=jnp.float32)

    sums, squares = [], []
    for g in range(act_frames):
        plain = jnp.zeros((1, C), jnp.float32)
        square = jnp.zeros((1, C), jnp.float32)
        for r in range(rows):
            part = first[g * padded : (g + 1) * padded, r * C : (r + 1) * C]
            plain = plain + jnp.sum(part, axis=0, keepdims=True)
            square = square + jnp.sum(part * part, axis=0, keepdims=True)
        sums.append(plain)
        squares.append(square)
    fill = [jnp.zeros((1, C), jnp.float32)] * (-(2 * act_frames) % 16)
    totals = group_sums(jnp.concatenate(sums + squares + fill, axis=0), matrix[...])
    size = float(rows * columns * WIDTH)
    mean = totals[:act_frames] / size
    variance = totals[act_frames : 2 * act_frames] / size - mean * mean
    scale = lax.rsqrt(variance + EPSILON) * flat_terms[0:1]
    shift = flat_terms[1:2] - mean * scale
    for g in range(act_frames):
        live = my_start - 2 + g >= 0
        scale_g = jnp.where(live, scale[g : g + 1], 0.0)
        shift_g = jnp.where(live, shift[g : g + 1], 0.0)
        for r in range(rows):
            part = first[g * padded : g * padded + columns, r * C : (r + 1) * C]
            act = silu(part * scale_g + shift_g)
            act = jnp.concatenate([act, jnp.zeros((stride - columns, C), jnp.float32)], axis=0)
            acts[g * stride : (g + 1) * stride, r * C : (r + 1) * C] = act.astype(jnp.bfloat16)

    kernel = [kernel_0.at[0], kernel_1.at[0], kernel_1.at[1]]
    span = frames * stride
    inside = lax.broadcasted_iota(jnp.int32, (half, stride), 1) < columns
    spans = {}
    for r in range(rows):
        spans.setdefault((max(0, r - 1), min(rows - 1, r + 1)), []).append(r)
    for (low, high), members in spans.items():
        places = range(low, high + 1)
        positions = jnp.concatenate(
            [
                acts[t * stride : t * stride + span, place * C : (place + 1) * C]
                for place in places
                for t in range(3)
            ],
            axis=1,
        )
        weights = jnp.concatenate(
            [
                jnp.concatenate(
                    [kernel[t][place - r + 1] for place in places for t in range(3)], axis=1
                )
                for r in members
            ],
            axis=0,
        )
        taps = lax.dot_general(
            weights, positions, (((1,), (1,)), ((), ())), preferred_element_type=jnp.float32
        )
        for m, r in enumerate(members):
            top = m * 3 * half
            for f in range(frames):
                left = f * stride
                tap = [
                    taps[top + s * half : top + (s + 1) * half, left : left + stride]
                    for s in range(3)
                ]
                value = tap[1] + pltpu.roll(tap[0], 1, 1) + pltpu.roll(tap[2], stride - 1, 1)
                second[r, f] = jnp.where(inside, value, 0.0)

    lane_at = lax.broadcasted_iota(jnp.int32, (half, LANES), 1)
    columns_of = jnp.zeros((half, LANES), jnp.float32)
    for f in range(frames):
        plain, square = second[0, f], second[0, f] * second[0, f]
        for r in range(1, rows):
            plain = plain + second[r, f]
            square = square + second[r, f] * second[r, f]
        columns_of = jnp.where(lane_at == f, jnp.sum(plain, axis=1, keepdims=True), columns_of)
        columns_of = jnp.where(
            lane_at == frames + f, jnp.sum(square, axis=1, keepdims=True), columns_of
        )
    high = columns_of.astype(jnp.bfloat16)
    rest = columns_of - high.astype(jnp.float32)
    middle = rest.astype(jnp.bfloat16)
    low = (rest - middle.astype(jnp.float32)).astype(jnp.bfloat16)
    matrix2 = matrix[:half, :half]
    totals = (
        jnp.dot(matrix2, high, preferred_element_type=jnp.float32)
        + jnp.dot(matrix2, middle, preferred_element_type=jnp.float32)
        + jnp.dot(matrix2, low, preferred_element_type=jnp.float32)
    )
    mean = totals / size
    variance = pltpu.roll(mean, LANES - frames, 1) - mean * mean
    scale = lax.rsqrt(variance + EPSILON) * tall_terms[0]
    shift = tall_terms[1] - mean * scale
    for f in range(frames):
        for inner in range(own_rows):
            part = second[lax.axis_index("band") * own_rows + inner, f]
            value = silu(part * scale[:, f : f + 1] + shift[:, f : f + 1])
            value = jnp.where(f < my_count, value, 0.0).astype(out.dtype)
            out[f, inner] = value[:, :columns]


def shards(latents, frame_counts, w_in, gain_in, shift_in, w_mid, gain_out, shift_out):
    frames, own_rows, flat = latents.shape
    columns = flat // LAT
    half = w_mid.shape[4]
    blocks, bands = lax.axis_size("block"), lax.axis_size("band")
    rows = own_rows * bands
    use_ring = small_slice(blocks, bands, own_rows, lax.axis_size("chan"))
    own = jnp.transpose(latents, (1, 0, 2))
    middle = jnp.transpose(w_mid, (0, 1, 2, 4, 3)).reshape(3, 3, 3 * half, C)
    kept, *prepared = prepare(
        (blocks, rows, own_rows, frames, use_ring),
        own,
        w_in,
        gain_in,
        shift_in,
        gain_out,
        shift_out,
        frame_counts,
        middle,
    )
    prepared.append(load_rest(middle))
    if use_ring:
        sources = exchange_ring(own, kept)
    else:
        gathered = lax.all_gather(kept, ("block", "band"), axis=0)
        sources = [gathered.reshape(-1, frames, flat)]
    pieces = tuple(a.shape[0] for a in sources)
    chunks = columns // COLS_IN_TILE
    slab = -(-(chunks + 1) // 8) * 8
    padded = -(-(columns + 1) // 16) * 16
    stride = -(-(columns + 1) // LANES) * LANES
    pairs = -(-rows // 2)
    cfg = (rows, frames, columns, pieces)
    vmem = pl.BlockSpec(memory_space=pltpu.VMEM)
    decoded = pl.pallas_call(
        functools.partial(body, cfg),
        out_shape=jax.ShapeDtypeStruct((frames, own_rows, half, columns), jnp.bfloat16),
        in_specs=[vmem] * (len(sources) + len(prepared)),
        out_specs=vmem,
        scratch_shapes=[
            pltpu.SMEM((8, LANES), jnp.int32),
            pltpu.VMEM((sum(pieces) * frames * slab, LANES), jnp.float32),
            pltpu.VMEM((pairs * (frames + HALO) * padded, LANES), jnp.float32),
            pltpu.VMEM(((frames + 2) * padded, rows * C), jnp.float32),
            pltpu.VMEM(((frames + 2) * stride, rows * C), jnp.bfloat16),
            pltpu.VMEM((rows, frames, half, stride), jnp.float32),
            pltpu.SemaphoreType.DMA,
        ],
        compiler_params=pltpu.CompilerParams(vmem_limit_bytes=32 * 1024 * 1024),
    )(*sources, *prepared)
    return jnp.transpose(decoded, (0, 1, 3, 2))


def small_slice(blocks, bands, own_rows, cores):
    return blocks == 4 and bands == 2 and own_rows == 1 and cores == 2


def solution(mesh):
    return jax.shard_map(
        shards,
        mesh=mesh,
        in_specs=(
            P(("video", "block"), "band", None),
            P("video"),
            P(),
            P(),
            P(),
            P(None, None, None, None, "chan"),
            P("chan"),
            P("chan"),
        ),
        out_specs=P(("video", "block"), "band", None, "chan"),
        check_vma=False,
    )
```

```python
import functools

import jax
import jax.numpy as jnp
from jax import lax
from jax.experimental import pallas as pl
from jax.experimental.pallas import tpu as pltpu
from jax.sharding import PartitionSpec as P


LAT = 16
C = 384
GROUPS = 32
WIDTH = C // GROUPS
EPSILON = 1e-06
LANES = 128
COLS_IN_TILE = LANES // LAT


FIRST_ROUND = (
    ((0, 1), (2, 0), (1, 0), (3, 1)),
    ((1, 1), (3, 0), (0, 0), (2, 0)),
)
SECOND_ROUND = (
    ((1, 0), (0, 0), (3, 1), (2, 0)),
    ((1, 0), (3, 0), (0, 0), (2, 1)),
)


def round_moves(sources):
    moves = []
    for core in range(2):
        for block in range(4):
            for band in range(2):
                from_block, turn = sources[core][block]
                source = (from_block * 2 + (band ^ turn)) * 2 + core
                moves.append((source, (block * 2 + band) * 2 + core))
    return moves


def held_pieces(core, block):
    return [(block, 0), FIRST_ROUND[core][block], FIRST_ROUND[1 - core][block]]


def all_pieces(core, block):
    pieces = held_pieces(core, block)
    for who in (core, 1 - core):
        from_block, turn = SECOND_ROUND[who][block]
        pieces += [(b, t ^ turn) for b, t in held_pieces(who, from_block)]
    return pieces


def choose(index, values):
    out = jnp.int32(values[0])
    for i, value in enumerate(values[1:], 1):
        out = jnp.where(index == i, value, out)
    return out


def piece_finder(bands, use_ring):
    block, band = lax.axis_index("block"), lax.axis_index("band")
    if not use_ring:
        return lambda owner, rank: owner * bands + rank
    mine = lax.axis_index("chan") * 4 + block
    places = []
    for owner in range(4):
        for turn in range(2):
            column = []
            for core in range(2):
                for at in range(4):
                    found = all_pieces(core, at)
                    column.append(found.index((owner, turn)) if (owner, turn) in found else 0)
            places.append(choose(mine, column))
    return lambda owner, rank: choose(owner * 2 + lax.rem(rank + band, 2), places)


def pack_body(*refs):
    out = refs[-1]
    for i, ref in enumerate(refs[:-1]):
        out[i] = ref[0]


def pack(*parts):
    vmem = pl.BlockSpec(memory_space=pltpu.VMEM)
    return pl.pallas_call(
        pack_body,
        out_shape=jax.ShapeDtypeStruct((len(parts),) + parts[0].shape[1:], parts[0].dtype),
        in_specs=[vmem] * len(parts),
        out_specs=vmem,
        compiler_params=pltpu.CompilerParams(vmem_limit_bytes=1024 * 1024),
    )(*parts)


def exchange_ring(latents, kept):
    axes = ("block", "band", "chan")
    swap = [(2 * n + c, 2 * n + 1 - c) for n in range(8) for c in range(2)]
    first = lax.ppermute(latents, axes, round_moves(FIRST_ROUND))
    second = lax.ppermute(first, axes, swap)
    held = pack(kept, first, second)
    third = lax.ppermute(held, axes, round_moves(SECOND_ROUND))
    fourth = lax.ppermute(third, axes, swap)
    return [kept, first, second, third, fourth]


def group_matrix(width):
    rows = lax.broadcasted_iota(jnp.int32, (width, width), 0)
    cols = lax.broadcasted_iota(jnp.int32, (width, width), 1)
    low = cols - lax.rem(cols, WIDTH)
    same = (rows >= low) & (rows < low + WIDTH)
    return jnp.where(same, 1.0, 0.0).astype(jnp.bfloat16)


def group_sums(sums, matrix):
    high = sums.astype(jnp.bfloat16)
    rest = sums - high.astype(jnp.float32)
    middle = rest.astype(jnp.bfloat16)
    low = (rest - middle.astype(jnp.float32)).astype(jnp.bfloat16)
    rows = sums.shape[0]
    parts = jnp.concatenate([high, middle, low], axis=0)
    out = jnp.dot(parts, matrix, preferred_element_type=jnp.float32)
    return out[:rows] + out[rows : 2 * rows] + out[2 * rows :]


def silu(u):
    half_u = 0.5 * u
    return half_u + half_u * jnp.tanh(half_u)


HALO = 4


def prepare_body(cfg, *refs):
    blocks, rows, own_rows, frames, use_ring = cfg
    latents, w_in, gain_in, shift_in, gain_out, shift_out, counts_in, w_mid = refs[:8]
    own, wide, matrix, flat_terms, tall_terms, table, kernel = refs[8:15]
    small, flat_parts, tall_parts, counts, sems = refs[15:]
    half = tall_terms.shape[1]
    depth = wide.shape[0] // 3
    copies = (
        (counts_in, counts),
        (latents, own),
        (w_in, small),
        (gain_in, flat_parts.at[0]),
        (shift_in, flat_parts.at[1]),
        (gain_out, tall_parts.at[0]),
        (shift_out, tall_parts.at[1]),
        (w_mid.at[: kernel.shape[0]], kernel),
    )
    loads = [pltpu.make_async_copy(a, b, sems.at[i]) for i, (a, b) in enumerate(copies)]
    for load in loads:
        load.start()
    wide[...] = jnp.zeros_like(wide)
    matrix[...] = group_matrix(C)
    eye = lax.broadcasted_iota(jnp.int32, (half, half), 0) == lax.broadcasted_iota(
        jnp.int32, (half, half), 1
    )
    block = lax.axis_index("block")
    find = piece_finder(rows // own_rows, use_ring)
    loads[0].wait()
    my_start = jnp.int32(0)
    for k in range(blocks):
        my_start = my_start + jnp.where(k < block, counts[k], 0)
    entries = []
    for f in range(HALO):
        wanted = my_start - HALO + f
        safe = jnp.maximum(wanted, 0)
        total, begin, owner = jnp.int32(0), jnp.int32(0), jnp.int32(0)
        for k in range(blocks):
            total = total + counts[k]
            past = safe >= total
            owner = owner + jnp.where(past, 1, 0)
            begin = jnp.where(past, total, begin)
        for r in range(rows):
            piece = find(owner, r // own_rows) * own_rows + r % own_rows
            entries.append(jnp.where(wanted >= 0, piece * frames + safe - begin, -1))
    for r in range(rows):
        piece = find(block, r // own_rows) * own_rows + r % own_rows
        entries.append(piece * frames)
    entries += [my_start, counts[block]]
    lane = lax.broadcasted_iota(jnp.int32, table.shape, 1)
    line = jnp.zeros(table.shape, jnp.int32)
    for i, entry in enumerate(entries):
        line = jnp.where(lane == i, entry, line)
    table[...] = line
    for load in loads[1:-1]:
        load.wait()
    for t in range(3):
        for place in range(rows):
            for r in range(rows):
                y = place - r + 1
                if 0 <= y <= 2:
                    top = t * depth + place * 64
                    wide[top : top + 3 * LAT, r * C : (r + 1) * C] = small[t, y]
    for i in range(2):
        flat_terms[i : i + 1] = flat_parts[i].reshape(1, C)
        spread = jnp.where(eye, tall_parts[i].reshape(1, half), 0.0)
        tall_terms[i] = jnp.broadcast_to(jnp.sum(spread, axis=1, keepdims=True), (half, LANES))
    loads[-1].wait()
    differences(rows, kernel.at[0])


def in_hbm(a):
    return pltpu.with_memory_space_constraint(a, pltpu.HBM)


def prepare(cfg, own, w_in, gain_in, shift_in, gain_out, shift_out, counts, middle):
    blocks, rows = cfg[:2]
    half = gain_out.shape[0]
    pairs = -(-rows // 2)
    small = (3, 3, 3 * LAT, C)
    operands = (
        own,
        w_in.reshape(small),
        gain_in,
        shift_in,
        gain_out,
        shift_out,
        counts,
        middle,
    )
    return pl.pallas_call(
        functools.partial(prepare_body, cfg),
        out_shape=(
            pltpu.VMEM(own.shape, own.dtype),
            pltpu.VMEM((3 * pairs * LANES, rows * C), jnp.bfloat16),
            pltpu.VMEM((C, C), jnp.bfloat16),
            pltpu.VMEM((8, C), jnp.float32),
            pltpu.VMEM((2, half, LANES), jnp.float32),
            pltpu.VMEM((8, LANES), jnp.int32),
            pltpu.VMEM((1,) + middle.shape[1:], middle.dtype),
        ),
        in_specs=[pl.BlockSpec(memory_space=pltpu.HBM)] * 8,
        out_specs=(pl.BlockSpec(memory_space=pltpu.VMEM),) * 7,
        scratch_shapes=[
            pltpu.VMEM(small, jnp.bfloat16),
            pltpu.VMEM((2, C), jnp.float32),
            pltpu.VMEM((2, half), jnp.float32),
            pltpu.SMEM((blocks,), jnp.int32),
            pltpu.SemaphoreType.DMA((8,)),
        ],
        compiler_params=pltpu.CompilerParams(vmem_limit_bytes=16 * 1024 * 1024),
    )(*[in_hbm(a) for a in operands])


def differences(rows, kernel):
    if rows == 2:
        kernel[0] = kernel[0] - kernel[1]
        kernel[2] = kernel[2] - kernel[1]


def load_body(rows, w_mid, kernel, sems):
    count = kernel.shape[0]
    loads = [
        pltpu.make_async_copy(w_mid.at[3 - count + i], kernel.at[i], sems.at[i])
        for i in range(count)
    ]
    for load in loads:
        load.start()
    for i, load in enumerate(loads):
        load.wait()
        differences(rows, kernel.at[i])


def load_rest(rows, middle):
    return pl.pallas_call(
        functools.partial(load_body, rows),
        out_shape=pltpu.VMEM((2,) + middle.shape[1:], middle.dtype),
        in_specs=[pl.BlockSpec(memory_space=pltpu.HBM)],
        out_specs=pl.BlockSpec(memory_space=pltpu.VMEM),
        scratch_shapes=[pltpu.SemaphoreType.DMA((2,))],
        compiler_params=pltpu.CompilerParams(vmem_limit_bytes=4 * 1024 * 1024),
    )(in_hbm(middle))


def body(cfg, *refs):
    rows, frames, columns, pieces = cfg
    n_arrays = len(pieces)
    sources = refs[:n_arrays]
    wide, matrix, flat_terms, tall_terms, table, kernel_0, kernel_1, out = refs[
        n_arrays : n_arrays + 8
    ]
    slabs, patches, first, acts, second = refs[n_arrays + 8 :]
    half = out.shape[2]
    chunks = columns // COLS_IN_TILE
    slab = -(-(chunks + 1) // 8) * 8
    padded = -(-(columns + 1) // 16) * 16
    stride = -(-(columns + 1) // LANES) * LANES
    lat_frames = frames + HALO
    act_frames = frames + 2
    pairs = -(-rows // 2)
    own_rows = out.shape[1]
    slabs[...] = jnp.zeros_like(slabs)
    at = 0
    for source, n in zip(sources, pieces):
        for p in range(n):
            values = source[p].astype(jnp.float32)
            for b in range(chunks):
                slabs[pl.ds(at * frames * slab + b, frames, stride=slab), :] = values[
                    :, b * LANES : (b + 1) * LANES
                ]
            at += 1

    line = table[0:1]
    entry = [line[0, i] for i in range((HALO + 1) * rows + 2)]
    my_start, my_count = entry[-2:]
    lane = lax.broadcasted_iota(jnp.int32, (slab, LANES), 1)
    patches[...] = jnp.zeros_like(patches)
    for f in range(lat_frames):
        planes = []
        for r in range(rows):
            if f < HALO:
                at = entry[f * rows + r]
                top = pl.multiple_of(jnp.maximum(at, 0) * slab, 8)
                planes.append(jnp.where(at >= 0, slabs[pl.ds(top, slab), :], 0.0))
            else:
                at = entry[HALO * rows + r] + (f - HALO)
                planes.append(slabs[pl.ds(pl.multiple_of(at * slab, 8), slab), :])
        if rows % 2:
            planes.append(jnp.zeros_like(planes[0]))
        for g in range(pairs):
            left, right = planes[2 * g], pltpu.roll(planes[2 * g + 1], 64, 1)
            for j in range(COLS_IN_TILE):
                begin_lane = LAT * (j - 1)
                a, b = left, right
                if j == 0:
                    a = jnp.where(lane >= LANES - LAT, pltpu.roll(left, 1, 0), left)
                    b = jnp.where(
                        (lane >= 64 - LAT) & (lane < 64), pltpu.roll(right, 1, 0), right
                    )
                if j == COLS_IN_TILE - 1:
                    a = jnp.where(lane < LAT, pltpu.roll(left, slab - 1, 0), left)
                    b = jnp.where(
                        (lane >= 64) & (lane < 64 + LAT), pltpu.roll(right, slab - 1, 0), right
                    )
                low = begin_lane % LANES
                if low + 64 <= LANES:
                    inside = (lane >= low) & (lane < low + 64)
                else:
                    inside = (lane >= low) | (lane < low + 64 - LANES)
                mixed = pltpu.roll(jnp.where(inside, a, b), (-begin_lane) % LANES, 1)
                patches[
                    pl.ds((g * lat_frames + f) * padded + j, chunks, stride=COLS_IN_TILE), :
                ] = mixed[:chunks]

    low_patches = patches[...].astype(jnp.bfloat16)
    stacked = jnp.concatenate(
        [
            low_patches[(g * lat_frames + t) * padded : (g * lat_frames + t + act_frames) * padded]
            for t in range(3)
            for g in range(pairs)
        ],
        axis=1,
    )
    first[...] = jnp.dot(stacked, wide[...], preferred_element_type=jnp.float32)

    sums, squares = [], []
    for g in range(act_frames):
        plain = jnp.zeros((1, C), jnp.float32)
        square = jnp.zeros((1, C), jnp.float32)
        for r in range(rows):
            part = first[g * padded : (g + 1) * padded, r * C : (r + 1) * C]
            plain = plain + jnp.sum(part, axis=0, keepdims=True)
            square = square + jnp.sum(part * part, axis=0, keepdims=True)
        sums.append(plain)
        squares.append(square)
    fill = [jnp.zeros((1, C), jnp.float32)] * (-(2 * act_frames) % 16)
    totals = group_sums(jnp.concatenate(sums + squares + fill, axis=0), matrix[...])
    size = float(rows * columns * WIDTH)
    mean = totals[:act_frames] / size
    variance = totals[act_frames : 2 * act_frames] / size - mean * mean
    scale = lax.rsqrt(variance + EPSILON) * flat_terms[0:1]
    shift = flat_terms[1:2] - mean * scale
    for g in range(act_frames):
        live = my_start - 2 + g >= 0
        scale_g = jnp.where(live, scale[g : g + 1], 0.0)
        shift_g = jnp.where(live, shift[g : g + 1], 0.0)
        for r in range(rows):
            part = first[g * padded : g * padded + columns, r * C : (r + 1) * C]
            act = silu(part * scale_g + shift_g)
            act = jnp.concatenate([act, jnp.zeros((stride - columns, C), jnp.float32)], axis=0)
            act = act.astype(jnp.bfloat16)
            acts[g * stride : (g + 1) * stride, r * C : (r + 1) * C] = act
            both = act if r == 0 else both + act
        if rows == 2:
            acts[g * stride : (g + 1) * stride, 2 * C :] = both

    kernel = [kernel_0.at[0], kernel_1.at[0], kernel_1.at[1]]
    inside = lax.broadcasted_iota(jnp.int32, (half, stride), 1) < columns
    lane_at = lax.broadcasted_iota(jnp.int32, (half, LANES), 1)
    columns_of = jnp.zeros((half, LANES), jnp.float32)
    group = 2 if frames % 2 == 0 else 1
    for f0 in range(0, frames, group):
        span = group * stride

        def product(taps_of, places_of):
            weights = jnp.concatenate(
                [kernel[t][y] for y in taps_of for t in range(3)], axis=1
            )
            positions = jnp.concatenate(
                [
                    acts[(f0 + t) * stride : (f0 + t) * stride + span, p * C : (p + 1) * C]
                    for p in places_of
                    for t in range(3)
                ],
                axis=1,
            )
            return lax.dot_general(
                weights, positions, (((1,), (1,)), ((), ())), preferred_element_type=jnp.float32
            )

        if rows == 2:
            shared = product([1], [2])
            taps = [shared + product([2], [1]), shared + product([0], [0])]
        else:
            taps = []
            for r in range(rows):
                places = range(max(0, r - 1), min(rows - 1, r + 1) + 1)
                taps.append(product([p - r + 1 for p in places], places))
        for f in range(f0, f0 + group):
            left = (f - f0) * stride
            plain = square = jnp.zeros((half, stride), jnp.float32)
            for r in range(rows):
                tap = [
                    taps[r][s * half : (s + 1) * half, left : left + stride] for s in range(3)
                ]
                value = tap[1] + pltpu.roll(tap[0], 1, 1) + pltpu.roll(tap[2], stride - 1, 1)
                value = jnp.where(inside, value, 0.0)
                second[r, f] = value
                plain = plain + value
                square = square + value * value
            columns_of = jnp.where(lane_at == f, jnp.sum(plain, axis=1, keepdims=True), columns_of)
            columns_of = jnp.where(
                lane_at == frames + f, jnp.sum(square, axis=1, keepdims=True), columns_of
            )

    high = columns_of.astype(jnp.bfloat16)
    rest = columns_of - high.astype(jnp.float32)
    middle = rest.astype(jnp.bfloat16)
    low = (rest - middle.astype(jnp.float32)).astype(jnp.bfloat16)
    matrix2 = matrix[:half, :half]
    totals = (
        jnp.dot(matrix2, high, preferred_element_type=jnp.float32)
        + jnp.dot(matrix2, middle, preferred_element_type=jnp.float32)
        + jnp.dot(matrix2, low, preferred_element_type=jnp.float32)
    )
    mean = totals / size
    variance = pltpu.roll(mean, LANES - frames, 1) - mean * mean
    scale = lax.rsqrt(variance + EPSILON) * tall_terms[0]
    shift = tall_terms[1] - mean * scale
    for f in range(frames):
        for inner in range(own_rows):
            part = second[lax.axis_index("band") * own_rows + inner, f]
            value = silu(part * scale[:, f : f + 1] + shift[:, f : f + 1])
            value = jnp.where(f < my_count, value, 0.0).astype(out.dtype)
            out[f, inner] = value[:, :columns]


def shards(latents, frame_counts, w_in, gain_in, shift_in, w_mid, gain_out, shift_out):
    frames, own_rows, flat = latents.shape
    columns = flat // LAT
    half = w_mid.shape[4]
    blocks, bands = lax.axis_size("block"), lax.axis_size("band")
    rows = own_rows * bands
    use_ring = small_slice(blocks, bands, own_rows, lax.axis_size("chan"))
    own = jnp.transpose(latents, (1, 0, 2))
    middle = jnp.transpose(w_mid, (0, 1, 2, 4, 3)).reshape(3, 3, 3 * half, C)
    kept, *prepared = prepare(
        (blocks, rows, own_rows, frames, use_ring),
        own,
        w_in,
        gain_in,
        shift_in,
        gain_out,
        shift_out,
        frame_counts,
        middle,
    )
    prepared.append(load_rest(rows, middle))
    if use_ring:
        sources = exchange_ring(own, kept)
    else:
        gathered = lax.all_gather(kept, ("block", "band"), axis=0)
        sources = [gathered.reshape(-1, frames, flat)]
    pieces = tuple(a.shape[0] for a in sources)
    chunks = columns // COLS_IN_TILE
    slab = -(-(chunks + 1) // 8) * 8
    padded = -(-(columns + 1) // 16) * 16
    stride = -(-(columns + 1) // LANES) * LANES
    pairs = -(-rows // 2)
    cfg = (rows, frames, columns, pieces)
    vmem = pl.BlockSpec(memory_space=pltpu.VMEM)
    decoded = pl.pallas_call(
        functools.partial(body, cfg),
        out_shape=jax.ShapeDtypeStruct((frames, own_rows, half, columns), jnp.bfloat16),
        in_specs=[vmem] * (len(sources) + len(prepared)),
        out_specs=vmem,
        scratch_shapes=[
            pltpu.VMEM((sum(pieces) * frames * slab, LANES), jnp.float32),
            pltpu.VMEM((pairs * (frames + HALO) * padded, LANES), jnp.float32),
            pltpu.VMEM(((frames + 2) * padded, rows * C), jnp.float32),
            pltpu.VMEM(((frames + 2) * stride, (rows + (rows == 2)) * C), jnp.bfloat16),
            pltpu.VMEM((rows, frames, half, stride), jnp.float32),
        ],
        compiler_params=pltpu.CompilerParams(vmem_limit_bytes=32 * 1024 * 1024),
    )(*sources, *prepared)
    return jnp.transpose(decoded, (0, 1, 3, 2))


def small_slice(blocks, bands, own_rows, cores):
    return blocks == 4 and bands == 2 and own_rows == 1 and cores == 2


def solution(mesh):
    return jax.shard_map(
        shards,
        mesh=mesh,
        in_specs=(
            P(("video", "block"), "band", None),
            P("video"),
            P(),
            P(),
            P(),
            P(None, None, None, None, "chan"),
            P("chan"),
            P("chan"),
        ),
        out_specs=P(("video", "block"), "band", None, "chan"),
        check_vma=False,
    )
```

```python
import functools

import jax
import jax.numpy as jnp
from jax import lax
from jax.experimental import pallas as pl
from jax.experimental.pallas import tpu as pltpu
from jax.sharding import PartitionSpec as P


LAT = 16
C = 384
GROUPS = 32
WIDTH = C // GROUPS
EPSILON = 1e-06
LANES = 128
COLS_IN_TILE = LANES // LAT


FIRST_ROUND = (
    ((0, 1), (2, 0), (1, 0), (3, 1)),
    ((1, 1), (3, 0), (0, 0), (2, 0)),
)
SECOND_ROUND = (
    ((1, 0), (0, 0), (3, 1), (2, 0)),
    ((1, 0), (3, 0), (0, 0), (2, 1)),
)


def round_moves(sources):
    moves = []
    for core in range(2):
        for block in range(4):
            for band in range(2):
                from_block, turn = sources[core][block]
                source = (from_block * 2 + (band ^ turn)) * 2 + core
                moves.append((source, (block * 2 + band) * 2 + core))
    return moves


def held_pieces(core, block):
    return [(block, 0), FIRST_ROUND[core][block], FIRST_ROUND[1 - core][block]]


def all_pieces(core, block):
    pieces = held_pieces(core, block)
    for who in (core, 1 - core):
        from_block, turn = SECOND_ROUND[who][block]
        pieces += [(b, t ^ turn) for b, t in held_pieces(who, from_block)]
    return pieces


def choose(index, values):
    out = jnp.int32(values[0])
    for i, value in enumerate(values[1:], 1):
        out = jnp.where(index == i, value, out)
    return out


def piece_finder(bands, use_ring):
    block, band = lax.axis_index("block"), lax.axis_index("band")
    if not use_ring:
        return lambda owner, rank: owner * bands + rank
    mine = lax.axis_index("chan") * 4 + block
    places = []
    for owner in range(4):
        for turn in range(2):
            column = []
            for core in range(2):
                for at in range(4):
                    found = all_pieces(core, at)
                    column.append(found.index((owner, turn)) if (owner, turn) in found else 0)
            places.append(choose(mine, column))
    return lambda owner, rank: choose(owner * 2 + lax.rem(rank + band, 2), places)


def pack_body(*refs):
    out = refs[-1]
    for i, ref in enumerate(refs[:-1]):
        out[i] = ref[0]


def pack(*parts):
    vmem = pl.BlockSpec(memory_space=pltpu.VMEM)
    return pl.pallas_call(
        pack_body,
        out_shape=jax.ShapeDtypeStruct((len(parts),) + parts[0].shape[1:], parts[0].dtype),
        in_specs=[vmem] * len(parts),
        out_specs=vmem,
        compiler_params=pltpu.CompilerParams(vmem_limit_bytes=1024 * 1024),
    )(*parts)


def exchange_ring(latents, kept):
    axes = ("block", "band", "chan")
    swap = [(2 * n + c, 2 * n + 1 - c) for n in range(8) for c in range(2)]
    first = lax.ppermute(latents, axes, round_moves(FIRST_ROUND))
    second = lax.ppermute(first, axes, swap)
    held = pack(kept, first, second)
    third = lax.ppermute(held, axes, round_moves(SECOND_ROUND))
    fourth = lax.ppermute(third, axes, swap)
    return [kept, first, second, third, fourth]


def group_matrix(width):
    rows = lax.broadcasted_iota(jnp.int32, (width, width), 0)
    cols = lax.broadcasted_iota(jnp.int32, (width, width), 1)
    low = cols - lax.rem(cols, WIDTH)
    same = (rows >= low) & (rows < low + WIDTH)
    return jnp.where(same, 1.0, 0.0).astype(jnp.bfloat16)


def group_sums(sums, matrix):
    high = sums.astype(jnp.bfloat16)
    rest = sums - high.astype(jnp.float32)
    middle = rest.astype(jnp.bfloat16)
    low = (rest - middle.astype(jnp.float32)).astype(jnp.bfloat16)
    rows = sums.shape[0]
    parts = jnp.concatenate([high, middle, low], axis=0)
    out = jnp.dot(parts, matrix, preferred_element_type=jnp.float32)
    return out[:rows] + out[rows : 2 * rows] + out[2 * rows :]


def half_silu(h):
    return h + h * jnp.tanh(h)


def group_columns(values, size):
    row = lax.broadcasted_iota(jnp.int32, (8, LANES), 0)
    groups = []
    for top in range(0, values.shape[0], 2 * WIDTH):
        a, b, c = (values[top + 8 * i : top + 8 * (i + 1)] for i in range(3))
        groups.append(a + jnp.where(row < 4, b, 0.0))
        groups.append(c + jnp.where(row < 4, 0.0, b))
    groups += [jnp.zeros((8, LANES), jnp.float32)] * (-len(groups) % 8)
    out = []
    for at in range(0, len(groups), 8):
        tiles = groups[at : at + 8]
        for step in (4, 2, 1):
            first_half = (row & step) == 0
            tiles = [
                jnp.where(first_half, x, y)
                + jnp.where(first_half, pltpu.roll(x, 8 - step, 0), pltpu.roll(y, step, 0))
                for x, y in zip(tiles[::2], tiles[1::2])
            ]
        out.append(jnp.sum(tiles[0], axis=1, keepdims=True) / size)
    return out


def group_rows(tiles, rows, lanes):
    row = lax.broadcasted_iota(jnp.int32, (8, lanes), 0)
    spread = []
    for n in range(rows // WIDTH):
        j = n % 8
        at = (j & 1) * 4 + (j & 2) + (j >> 2)
        spread.append(jnp.broadcast_to(tiles[n // 8][at : at + 1, :], (8, lanes)))
    out = []
    for a, b in zip(spread[::2], spread[1::2]):
        out += [a, jnp.where(row < 4, a, b), b]
    return jnp.concatenate(out, axis=0)


HALO = 4


def prepare_body(cfg, *refs):
    blocks, rows, own_rows, frames, use_ring = cfg
    latents, w_in, gain_in, shift_in, gain_out, shift_out, counts_in, w_mid = refs[:8]
    own, wide, matrix, flat_terms, tall_terms, table, kernel = refs[8:15]
    small, flat_parts, tall_parts, counts, sems = refs[15:]
    half = tall_terms.shape[1]
    depth = wide.shape[0] // 3
    copies = (
        (counts_in, counts),
        (latents, own),
        (w_in, small),
        (gain_in, flat_parts.at[0]),
        (shift_in, flat_parts.at[1]),
        (gain_out, tall_parts.at[0]),
        (shift_out, tall_parts.at[1]),
        (w_mid.at[: kernel.shape[0]], kernel),
    )
    loads = [pltpu.make_async_copy(a, b, sems.at[i]) for i, (a, b) in enumerate(copies)]
    for load in loads:
        load.start()
    wide[...] = jnp.zeros_like(wide)
    matrix[...] = group_matrix(C)
    eye = lax.broadcasted_iota(jnp.int32, (half, half), 0) == lax.broadcasted_iota(
        jnp.int32, (half, half), 1
    )
    block = lax.axis_index("block")
    find = piece_finder(rows // own_rows, use_ring)
    loads[0].wait()
    my_start = jnp.int32(0)
    for k in range(blocks):
        my_start = my_start + jnp.where(k < block, counts[k], 0)
    entries = []
    for f in range(HALO):
        wanted = my_start - HALO + f
        safe = jnp.maximum(wanted, 0)
        total, begin, owner = jnp.int32(0), jnp.int32(0), jnp.int32(0)
        for k in range(blocks):
            total = total + counts[k]
            past = safe >= total
            owner = owner + jnp.where(past, 1, 0)
            begin = jnp.where(past, total, begin)
        for r in range(rows):
            piece = find(owner, r // own_rows) * own_rows + r % own_rows
            entries.append(jnp.where(wanted >= 0, piece * frames + safe - begin, -1))
    for r in range(rows):
        piece = find(block, r // own_rows) * own_rows + r % own_rows
        entries.append(piece * frames)
    entries += [my_start, counts[block]]
    lane = lax.broadcasted_iota(jnp.int32, table.shape, 1)
    line = jnp.zeros(table.shape, jnp.int32)
    for i, entry in enumerate(entries):
        line = jnp.where(lane == i, entry, line)
    table[...] = line
    for load in loads[1:-1]:
        load.wait()
    for t in range(3):
        for place in range(rows):
            for r in range(rows):
                y = place - r + 1
                if 0 <= y <= 2:
                    top = t * depth + place * 64
                    wide[top : top + 3 * LAT, r * C : (r + 1) * C] = small[t, y]
    for i in range(2):
        flat_terms[i : i + 1] = 0.5 * flat_parts[i].reshape(1, C)
        spread = jnp.where(eye, 0.5 * tall_parts[i].reshape(1, half), 0.0)
        tall_terms[i] = jnp.broadcast_to(jnp.sum(spread, axis=1, keepdims=True), (half, LANES))
    loads[-1].wait()
    differences(rows, kernel.at[0])


def in_hbm(a):
    return pltpu.with_memory_space_constraint(a, pltpu.HBM)


def prepare(cfg, own, w_in, gain_in, shift_in, gain_out, shift_out, counts, middle):
    blocks, rows = cfg[:2]
    half = gain_out.shape[0]
    pairs = -(-rows // 2)
    small = (3, 3, 3 * LAT, C)
    operands = (
        own,
        w_in.reshape(small),
        gain_in,
        shift_in,
        gain_out,
        shift_out,
        counts,
        middle,
    )
    return pl.pallas_call(
        functools.partial(prepare_body, cfg),
        out_shape=(
            pltpu.VMEM(own.shape, own.dtype),
            pltpu.VMEM((3 * pairs * LANES, rows * C), jnp.bfloat16),
            pltpu.VMEM((C, C), jnp.bfloat16),
            pltpu.VMEM((8, C), jnp.float32),
            pltpu.VMEM((2, half, LANES), jnp.float32),
            pltpu.VMEM((8, LANES), jnp.int32),
            pltpu.VMEM((1,) + middle.shape[1:], middle.dtype),
        ),
        in_specs=[pl.BlockSpec(memory_space=pltpu.HBM)] * 8,
        out_specs=(pl.BlockSpec(memory_space=pltpu.VMEM),) * 7,
        scratch_shapes=[
            pltpu.VMEM(small, jnp.bfloat16),
            pltpu.VMEM((2, C), jnp.float32),
            pltpu.VMEM((2, half), jnp.float32),
            pltpu.SMEM((blocks,), jnp.int32),
            pltpu.SemaphoreType.DMA((8,)),
        ],
        compiler_params=pltpu.CompilerParams(vmem_limit_bytes=16 * 1024 * 1024),
    )(*[in_hbm(a) for a in operands])


def differences(rows, kernel):
    if rows == 2:
        kernel[0] = kernel[0] - kernel[1]
        kernel[2] = kernel[2] - kernel[1]


def load_body(rows, w_mid, kernel, sems):
    count = kernel.shape[0]
    loads = [
        pltpu.make_async_copy(w_mid.at[3 - count + i], kernel.at[i], sems.at[i])
        for i in range(count)
    ]
    for load in loads:
        load.start()
    for i, load in enumerate(loads):
        load.wait()
        differences(rows, kernel.at[i])


def load_rest(rows, middle):
    return pl.pallas_call(
        functools.partial(load_body, rows),
        out_shape=pltpu.VMEM((2,) + middle.shape[1:], middle.dtype),
        in_specs=[pl.BlockSpec(memory_space=pltpu.HBM)],
        out_specs=pl.BlockSpec(memory_space=pltpu.VMEM),
        scratch_shapes=[pltpu.SemaphoreType.DMA((2,))],
        compiler_params=pltpu.CompilerParams(vmem_limit_bytes=4 * 1024 * 1024),
    )(in_hbm(middle))


def body(cfg, *refs):
    rows, frames, columns, pieces = cfg
    n_arrays = len(pieces)
    sources = refs[:n_arrays]
    wide, matrix, flat_terms, tall_terms, table, kernel_0, kernel_1, out = refs[
        n_arrays : n_arrays + 8
    ]
    slabs, patches, first, acts = refs[n_arrays + 8 :]
    half = out.shape[2]
    chunks = columns // COLS_IN_TILE
    slab = -(-(chunks + 1) // 8) * 8
    padded = -(-(columns + 1) // 16) * 16
    stride = -(-(columns + 1) // LANES) * LANES
    lat_frames = frames + HALO
    pairs = -(-rows // 2)
    own_rows = out.shape[1]
    at = 0
    for source, n in zip(sources, pieces):
        for p in range(n):
            values = source[p].astype(jnp.float32)
            for b in range(chunks):
                slabs[pl.ds(at * frames * slab + b, frames, stride=slab), :] = values[
                    :, b * LANES : (b + 1) * LANES
                ]
            for b in range(chunks, slab):
                slabs[pl.ds(at * frames * slab + b, frames, stride=slab), :] = jnp.zeros(
                    (frames, LANES), jnp.float32
                )
            at += 1

    line = table[0:1]
    entry = [line[0, i] for i in range((HALO + 1) * rows + 2)]
    my_start, my_count = entry[-2:]
    lane = lax.broadcasted_iota(jnp.int32, (slab, LANES), 1)
    for i in range(pairs * lat_frames):
        patches[i * padded + columns : (i + 1) * padded] = jnp.zeros(
            (padded - columns, LANES), jnp.float32
        )
    for f in range(lat_frames):
        planes = []
        for r in range(rows):
            if f < HALO:
                at = entry[f * rows + r]
                top = pl.multiple_of(jnp.maximum(at, 0) * slab, 8)
                planes.append(jnp.where(at >= 0, slabs[pl.ds(top, slab), :], 0.0))
            else:
                at = entry[HALO * rows + r] + (f - HALO)
                planes.append(slabs[pl.ds(pl.multiple_of(at * slab, 8), slab), :])
        if rows % 2:
            planes.append(jnp.zeros_like(planes[0]))
        for g in range(pairs):
            left, right = planes[2 * g], pltpu.roll(planes[2 * g + 1], 64, 1)
            for j in range(COLS_IN_TILE):
                begin_lane = LAT * (j - 1)
                a, b = left, right
                if j == 0:
                    a = jnp.where(lane >= LANES - LAT, pltpu.roll(left, 1, 0), left)
                    b = jnp.where(
                        (lane >= 64 - LAT) & (lane < 64), pltpu.roll(right, 1, 0), right
                    )
                if j == COLS_IN_TILE - 1:
                    a = jnp.where(lane < LAT, pltpu.roll(left, slab - 1, 0), left)
                    b = jnp.where(
                        (lane >= 64) & (lane < 64 + LAT), pltpu.roll(right, slab - 1, 0), right
                    )
                low = begin_lane % LANES
                if low + 64 <= LANES:
                    inside = (lane >= low) & (lane < low + 64)
                else:
                    inside = (lane >= low) | (lane < low + 64 - LANES)
                mixed = pltpu.roll(jnp.where(inside, a, b), (-begin_lane) % LANES, 1)
                patches[
                    pl.ds((g * lat_frames + f) * padded + j, chunks, stride=COLS_IN_TILE), :
                ] = mixed[:chunks]

    low_patches = patches[...].astype(jnp.bfloat16)
    size = float(rows * columns * WIDTH)

    def front(g0, g1):
        stacked = jnp.concatenate(
            [
                low_patches[
                    (g * lat_frames + t + g0) * padded : (g * lat_frames + t + g1) * padded
                ]
                for t in range(3)
                for g in range(pairs)
            ],
            axis=1,
        )
        first[g0 * padded : g1 * padded] = jnp.dot(
            stacked, wide[...], preferred_element_type=jnp.float32
        )
        sums, squares = [], []
        for g in range(g0, g1):
            plain = jnp.zeros((1, C), jnp.float32)
            square = jnp.zeros((1, C), jnp.float32)
            for r in range(rows):
                part = first[g * padded : (g + 1) * padded, r * C : (r + 1) * C]
                plain = plain + jnp.sum(part, axis=0, keepdims=True)
                square = square + jnp.sum(part * part, axis=0, keepdims=True)
            sums.append(plain)
            squares.append(square)
        n = g1 - g0
        fill = [jnp.zeros((1, C), jnp.float32)] * (-(2 * n) % 16)
        totals = group_sums(jnp.concatenate(sums + squares + fill, axis=0), matrix[...])
        mean = totals[:n] / size
        variance = totals[n : 2 * n] / size - mean * mean
        scale = lax.rsqrt(variance + EPSILON) * flat_terms[0:1]
        shift = flat_terms[1:2] - mean * scale
        for g in range(g0, g1):
            scale_g, shift_g = scale[g - g0 : g - g0 + 1], shift[g - g0 : g - g0 + 1]
            if g < 2:
                live = my_start - 2 + g >= 0
                scale_g, shift_g = jnp.where(live, scale_g, 0.0), jnp.where(live, shift_g, 0.0)
            for r in range(rows):
                part = first[g * padded : g * padded + columns, r * C : (r + 1) * C]
                act = half_silu(part * scale_g + shift_g)
                act = jnp.concatenate([act, jnp.zeros((stride - columns, C), jnp.float32)], axis=0)
                act = act.astype(jnp.bfloat16)
                acts[g * stride : (g + 1) * stride, r * C : (r + 1) * C] = act
                both = act if r == 0 else both + act
            if rows == 2:
                acts[g * stride : (g + 1) * stride, 2 * C :] = both

    kernel = [kernel_0.at[0], kernel_1.at[0], kernel_1.at[1]]
    inside = lax.broadcasted_iota(jnp.int32, (half, stride), 1) < columns
    group = 2 if frames % 2 == 0 else 1
    span = group * stride

    def terms(y, place):
        return [(y, place, t, c) for t in range(3) for c in range(C // LANES)]

    def product(f0, parts):
        weights = jnp.concatenate(
            [kernel[t][y][:, c * LANES : (c + 1) * LANES] for y, _, t, c in parts], axis=1
        )
        positions = jnp.concatenate(
            [
                acts[
                    (f0 + t) * stride : (f0 + t) * stride + span,
                    p * C + c * LANES : p * C + (c + 1) * LANES,
                ]
                for _, p, t, c in parts
            ],
            axis=1,
        )
        return lax.dot_general(
            weights, positions, (((1,), (1,)), ((), ())), preferred_element_type=jnp.float32
        )

    def back(f0):
        if rows == 2:
            middle = terms(1, 2)
            keep = len(middle) // 2 * 2
            shared = product(f0, middle[:keep])
            taps = [
                shared + product(f0, terms(2, 1) + middle[keep:]),
                shared + product(f0, terms(0, 0) + middle[keep:]),
            ]
        else:
            taps = []
            for r in range(rows):
                places = range(max(0, r - 1), min(rows - 1, r + 1) + 1)
                taps.append(product(f0, [q for p in places for q in terms(p - r + 1, p)]))
        band = lax.axis_index("band")
        for i in range(group):
            plain = square = jnp.zeros((half, stride), jnp.float32)
            own = [jnp.zeros((half, stride), jnp.float32)] * own_rows
            for r in range(rows):
                tap = [
                    taps[r][s * half : (s + 1) * half, i * stride : (i + 1) * stride]
                    for s in range(3)
                ]
                value = tap[1] + pltpu.roll(tap[0], 1, 1) + pltpu.roll(tap[2], stride - 1, 1)
                value = jnp.where(inside, value, 0.0)
                plain = plain + value
                square = square + value * value
                own = [
                    value if r == 0 else jnp.where(band * own_rows + inner == r, value, own[inner])
                    for inner in range(own_rows)
                ]
            mean = group_columns(plain, size)
            power = group_columns(square, size)
            inverse = [lax.rsqrt(p - m * m + EPSILON) for p, m in zip(power, mean)]
            scale = group_rows(inverse, half, stride) * tall_terms[0]
            shift = tall_terms[1] - group_rows(mean, half, stride) * scale
            for inner in range(own_rows):
                value = half_silu(own[inner] * scale + shift)
                value = jnp.where(f0 + i < my_count, value, 0.0).astype(out.dtype)
                out[f0 + i, inner] = value[:, :columns]

    front(0, frames + 2)
    for f0 in range(0, frames, group):
        back(f0)


def shards(latents, frame_counts, w_in, gain_in, shift_in, w_mid, gain_out, shift_out):
    frames, own_rows, flat = latents.shape
    columns = flat // LAT
    half = w_mid.shape[4]
    blocks, bands = lax.axis_size("block"), lax.axis_size("band")
    rows = own_rows * bands
    use_ring = small_slice(blocks, bands, own_rows, lax.axis_size("chan"))
    own = jnp.transpose(latents, (1, 0, 2))
    middle = jnp.transpose(w_mid, (0, 1, 2, 4, 3)).reshape(3, 3, 3 * half, C)
    kept, *prepared = prepare(
        (blocks, rows, own_rows, frames, use_ring),
        own,
        w_in,
        gain_in,
        shift_in,
        gain_out,
        shift_out,
        frame_counts,
        middle,
    )
    prepared.append(load_rest(rows, middle))
    if use_ring:
        sources = exchange_ring(own, kept)
    else:
        gathered = lax.all_gather(kept, ("block", "band"), axis=0)
        sources = [gathered.reshape(-1, frames, flat)]
    pieces = tuple(a.shape[0] for a in sources)
    chunks = columns // COLS_IN_TILE
    slab = -(-(chunks + 1) // 8) * 8
    padded = -(-(columns + 1) // 16) * 16
    stride = -(-(columns + 1) // LANES) * LANES
    pairs = -(-rows // 2)
    cfg = (rows, frames, columns, pieces)
    vmem = pl.BlockSpec(memory_space=pltpu.VMEM)
    decoded = pl.pallas_call(
        functools.partial(body, cfg),
        out_shape=jax.ShapeDtypeStruct((frames, own_rows, half, columns), jnp.bfloat16),
        in_specs=[vmem] * (len(sources) + len(prepared)),
        out_specs=vmem,
        scratch_shapes=[
            pltpu.VMEM((sum(pieces) * frames * slab, LANES), jnp.float32),
            pltpu.VMEM((pairs * (frames + HALO) * padded, LANES), jnp.float32),
            pltpu.VMEM(((frames + 2) * padded, rows * C), jnp.float32),
            pltpu.VMEM(((frames + 2) * stride, (rows + (rows == 2)) * C), jnp.bfloat16),
        ],
        compiler_params=pltpu.CompilerParams(vmem_limit_bytes=32 * 1024 * 1024),
    )(*sources, *prepared)
    return jnp.transpose(decoded, (0, 1, 3, 2))


def small_slice(blocks, bands, own_rows, cores):
    return blocks == 4 and bands == 2 and own_rows == 1 and cores == 2


def solution(mesh):
    return jax.shard_map(
        shards,
        mesh=mesh,
        in_specs=(
            P(("video", "block"), "band", None),
            P("video"),
            P(),
            P(),
            P(),
            P(None, None, None, None, "chan"),
            P("chan"),
            P("chan"),
        ),
        out_specs=P(("video", "block"), "band", None, "chan"),
        check_vma=False,
    )
```

```python
import functools

import jax
import jax.numpy as jnp
from jax import lax
from jax.experimental import pallas as pl
from jax.experimental.pallas import tpu as pltpu
from jax.sharding import PartitionSpec as P


LAT = 16
C = 384
GROUPS = 32
WIDTH = C // GROUPS
EPSILON = 1e-06
LANES = 128
COLS_IN_TILE = LANES // LAT


FIRST_ROUND = (
    ((0, 1), (2, 0), (1, 0), (3, 1)),
    ((1, 1), (3, 0), (0, 0), (2, 0)),
)
SECOND_ROUND = (
    ((1, 0), (0, 0), (3, 1), (2, 0)),
    ((1, 0), (3, 0), (0, 0), (2, 1)),
)


def round_moves(sources):
    moves = []
    for core in range(2):
        for block in range(4):
            for band in range(2):
                from_block, turn = sources[core][block]
                source = (from_block * 2 + (band ^ turn)) * 2 + core
                moves.append((source, (block * 2 + band) * 2 + core))
    return moves


def held_pieces(core, block):
    return [(block, 0), FIRST_ROUND[core][block], FIRST_ROUND[1 - core][block]]


def all_pieces(core, block):
    pieces = held_pieces(core, block)
    for who in (core, 1 - core):
        from_block, turn = SECOND_ROUND[who][block]
        pieces += [(b, t ^ turn) for b, t in held_pieces(who, from_block)]
    return pieces


def choose(index, values):
    out = jnp.int32(values[0])
    for i, value in enumerate(values[1:], 1):
        out = jnp.where(index == i, value, out)
    return out


def piece_finder(bands, use_ring):
    block, band = lax.axis_index("block"), lax.axis_index("band")
    if not use_ring:
        return lambda owner, rank: owner * bands + rank
    mine = lax.axis_index("chan") * 4 + block
    places = []
    for owner in range(4):
        for turn in range(2):
            column = []
            for core in range(2):
                for at in range(4):
                    found = all_pieces(core, at)
                    column.append(found.index((owner, turn)) if (owner, turn) in found else 0)
            places.append(choose(mine, column))
    return lambda owner, rank: choose(owner * 2 + lax.rem(rank + band, 2), places)


def pack_body(*refs):
    out = refs[-1]
    for i, ref in enumerate(refs[:-1]):
        out[i] = ref[0]


def pack(*parts):
    vmem = pl.BlockSpec(memory_space=pltpu.VMEM)
    return pl.pallas_call(
        pack_body,
        out_shape=jax.ShapeDtypeStruct((len(parts),) + parts[0].shape[1:], parts[0].dtype),
        in_specs=[vmem] * len(parts),
        out_specs=vmem,
        compiler_params=pltpu.CompilerParams(vmem_limit_bytes=1024 * 1024),
    )(*parts)


def exchange_ring(latents, kept):
    axes = ("block", "band", "chan")
    swap = [(2 * n + c, 2 * n + 1 - c) for n in range(8) for c in range(2)]
    first = lax.ppermute(latents, axes, round_moves(FIRST_ROUND))
    second = lax.ppermute(first, axes, swap)
    held = pack(kept, first, second)
    third = lax.ppermute(held, axes, round_moves(SECOND_ROUND))
    fourth = lax.ppermute(third, axes, swap)
    return [kept, first, second, third, fourth]


def group_matrix(width):
    rows = lax.broadcasted_iota(jnp.int32, (width, width), 0)
    cols = lax.broadcasted_iota(jnp.int32, (width, width), 1)
    low = cols - lax.rem(cols, WIDTH)
    same = (rows >= low) & (rows < low + WIDTH)
    return jnp.where(same, 1.0, 0.0).astype(jnp.bfloat16)


def group_sums(sums, matrix):
    high = sums.astype(jnp.bfloat16)
    rest = sums - high.astype(jnp.float32)
    middle = rest.astype(jnp.bfloat16)
    low = (rest - middle.astype(jnp.float32)).astype(jnp.bfloat16)
    rows = sums.shape[0]
    parts = jnp.concatenate([high, middle, low], axis=0)
    out = jnp.dot(parts, matrix, preferred_element_type=jnp.float32)
    return out[:rows] + out[rows : 2 * rows] + out[2 * rows :]


def half_silu(h):
    return h + h * jnp.tanh(h)


def group_columns(values, size):
    row = lax.broadcasted_iota(jnp.int32, (8, LANES), 0)
    groups = []
    for top in range(0, values.shape[0], 2 * WIDTH):
        a, b, c = (values[top + 8 * i : top + 8 * (i + 1)] for i in range(3))
        groups.append(a + jnp.where(row < 4, b, 0.0))
        groups.append(c + jnp.where(row < 4, 0.0, b))
    groups += [jnp.zeros((8, LANES), jnp.float32)] * (-len(groups) % 8)
    out = []
    for at in range(0, len(groups), 8):
        tiles = groups[at : at + 8]
        for step in (4, 2, 1):
            first_half = (row & step) == 0
            tiles = [
                jnp.where(first_half, x, y)
                + jnp.where(first_half, pltpu.roll(x, 8 - step, 0), pltpu.roll(y, step, 0))
                for x, y in zip(tiles[::2], tiles[1::2])
            ]
        out.append(jnp.sum(tiles[0], axis=1, keepdims=True) / size)
    return out


def group_rows(tiles, rows, lanes):
    row = lax.broadcasted_iota(jnp.int32, (8, lanes), 0)
    spread = []
    for n in range(rows // WIDTH):
        j = n % 8
        at = (j & 1) * 4 + (j & 2) + (j >> 2)
        spread.append(jnp.broadcast_to(tiles[n // 8][at : at + 1, :], (8, lanes)))
    out = []
    for a, b in zip(spread[::2], spread[1::2]):
        out += [a, jnp.where(row < 4, a, b), b]
    return jnp.concatenate(out, axis=0)


HALO = 4


def prepare_body(cfg, *refs):
    blocks, rows, own_rows, frames, use_ring = cfg
    latents, w_in, gain_in, shift_in, gain_out, shift_out, counts_in, w_mid = refs[:8]
    own, wide, matrix, flat_terms, tall_terms, table, kernel = refs[8:15]
    small, flat_parts, tall_parts, counts, sems = refs[15:]
    half = tall_terms.shape[1]
    depth = wide.shape[0] // 3
    copies = (
        (counts_in, counts),
        (latents, own),
        (w_in, small),
        (gain_in, flat_parts.at[0]),
        (shift_in, flat_parts.at[1]),
        (gain_out, tall_parts.at[0]),
        (shift_out, tall_parts.at[1]),
        (w_mid.at[: kernel.shape[0]], kernel),
    )
    loads = [pltpu.make_async_copy(a, b, sems.at[i]) for i, (a, b) in enumerate(copies)]
    for load in loads:
        load.start()
    wide[...] = jnp.zeros_like(wide)
    matrix[...] = group_matrix(C)
    eye = lax.broadcasted_iota(jnp.int32, (half, half), 0) == lax.broadcasted_iota(
        jnp.int32, (half, half), 1
    )
    block = lax.axis_index("block")
    find = piece_finder(rows // own_rows, use_ring)
    loads[0].wait()
    my_start = jnp.int32(0)
    for k in range(blocks):
        my_start = my_start + jnp.where(k < block, counts[k], 0)
    entries = []
    for f in range(HALO):
        wanted = my_start - HALO + f
        safe = jnp.maximum(wanted, 0)
        total, begin, owner = jnp.int32(0), jnp.int32(0), jnp.int32(0)
        for k in range(blocks):
            total = total + counts[k]
            past = safe >= total
            owner = owner + jnp.where(past, 1, 0)
            begin = jnp.where(past, total, begin)
        for r in range(rows):
            piece = find(owner, r // own_rows) * own_rows + r % own_rows
            entries.append(jnp.where(wanted >= 0, piece * frames + safe - begin, -1))
    for r in range(rows):
        piece = find(block, r // own_rows) * own_rows + r % own_rows
        entries.append(piece * frames)
    entries += [my_start, counts[block]]
    lane = lax.broadcasted_iota(jnp.int32, table.shape, 1)
    line = jnp.zeros(table.shape, jnp.int32)
    for i, entry in enumerate(entries):
        line = jnp.where(lane == i, entry, line)
    table[...] = line
    for load in loads[1:-1]:
        load.wait()
    for t in range(3):
        for place in range(rows):
            for r in range(rows):
                y = place - r + 1
                if 0 <= y <= 2:
                    top = t * depth + place * 64
                    wide[top : top + 3 * LAT, r * C : (r + 1) * C] = small[t, y]
    for i in range(2):
        flat_terms[i : i + 1] = 0.5 * flat_parts[i].reshape(1, C)
        spread = jnp.where(eye, 0.5 * tall_parts[i].reshape(1, half), 0.0)
        tall_terms[i] = jnp.broadcast_to(jnp.sum(spread, axis=1, keepdims=True), (half, LANES))
    loads[-1].wait()
    differences(rows, kernel.at[0])


def in_hbm(a):
    return pltpu.with_memory_space_constraint(a, pltpu.HBM)


def prepare(cfg, own, w_in, gain_in, shift_in, gain_out, shift_out, counts, middle):
    blocks, rows = cfg[:2]
    half = gain_out.shape[0]
    pairs = -(-rows // 2)
    small = (3, 3, 3 * LAT, C)
    operands = (
        own,
        w_in.reshape(small),
        gain_in,
        shift_in,
        gain_out,
        shift_out,
        counts,
        middle,
    )
    return pl.pallas_call(
        functools.partial(prepare_body, cfg),
        out_shape=(
            pltpu.VMEM(own.shape, own.dtype),
            pltpu.VMEM((3 * pairs * LANES, rows * C), jnp.bfloat16),
            pltpu.VMEM((C, C), jnp.bfloat16),
            pltpu.VMEM((8, C), jnp.float32),
            pltpu.VMEM((2, half, LANES), jnp.float32),
            pltpu.VMEM((8, LANES), jnp.int32),
            pltpu.VMEM((1,) + middle.shape[1:], middle.dtype),
        ),
        in_specs=[pl.BlockSpec(memory_space=pltpu.HBM)] * 8,
        out_specs=(pl.BlockSpec(memory_space=pltpu.VMEM),) * 7,
        scratch_shapes=[
            pltpu.VMEM(small, jnp.bfloat16),
            pltpu.VMEM((2, C), jnp.float32),
            pltpu.VMEM((2, half), jnp.float32),
            pltpu.SMEM((blocks,), jnp.int32),
            pltpu.SemaphoreType.DMA((8,)),
        ],
        compiler_params=pltpu.CompilerParams(vmem_limit_bytes=16 * 1024 * 1024),
    )(*[in_hbm(a) for a in operands])


def differences(rows, kernel):
    if rows == 2:
        kernel[0] = kernel[0] - kernel[1]
        kernel[2] = kernel[2] - kernel[1]


def load_body(rows, w_mid, kernel, sems):
    count = kernel.shape[0]
    loads = [
        pltpu.make_async_copy(w_mid.at[3 - count + i], kernel.at[i], sems.at[i])
        for i in range(count)
    ]
    for load in loads:
        load.start()
    for i, load in enumerate(loads):
        load.wait()
        differences(rows, kernel.at[i])


def load_rest(rows, middle):
    return pl.pallas_call(
        functools.partial(load_body, rows),
        out_shape=pltpu.VMEM((2,) + middle.shape[1:], middle.dtype),
        in_specs=[pl.BlockSpec(memory_space=pltpu.HBM)],
        out_specs=pl.BlockSpec(memory_space=pltpu.VMEM),
        scratch_shapes=[pltpu.SemaphoreType.DMA((2,))],
        compiler_params=pltpu.CompilerParams(vmem_limit_bytes=4 * 1024 * 1024),
    )(in_hbm(middle))


def body(cfg, *refs):
    rows, frames, columns, pieces = cfg
    n_arrays = len(pieces)
    sources = refs[:n_arrays]
    wide, matrix, flat_terms, tall_terms, table, kernel_0, kernel_1, out = refs[
        n_arrays : n_arrays + 8
    ]
    slabs, patches, first, acts = refs[n_arrays + 8 :]
    half = out.shape[2]
    chunks = columns // COLS_IN_TILE
    slab = -(-(chunks + 1) // 8) * 8
    padded = -(-(columns + 1) // 16) * 16
    stride = -(-(columns + 1) // LANES) * LANES
    lat_frames = frames + HALO
    pairs = -(-rows // 2)
    own_rows = out.shape[1]
    at = 0
    for source, n in zip(sources, pieces):
        for p in range(n):
            values = source[p].astype(jnp.float32)
            for b in range(chunks):
                slabs[pl.ds(at * frames * slab + b, frames, stride=slab), :] = values[
                    :, b * LANES : (b + 1) * LANES
                ]
            for b in range(chunks, slab):
                slabs[pl.ds(at * frames * slab + b, frames, stride=slab), :] = jnp.zeros(
                    (frames, LANES), jnp.float32
                )
            at += 1

    line = table[0:1]
    entry = [line[0, i] for i in range((HALO + 1) * rows + 2)]
    my_start, my_count = entry[-2:]
    lane = lax.broadcasted_iota(jnp.int32, (slab, LANES), 1)
    for i in range(pairs * lat_frames):
        patches[i * padded + columns : (i + 1) * padded] = jnp.zeros(
            (padded - columns, LANES), jnp.float32
        )
    for f in range(lat_frames):
        planes = []
        for r in range(rows):
            if f < HALO:
                at = entry[f * rows + r]
                top = pl.multiple_of(jnp.maximum(at, 0) * slab, 8)
                planes.append(jnp.where(at >= 0, slabs[pl.ds(top, slab), :], 0.0))
            else:
                at = entry[HALO * rows + r] + (f - HALO)
                planes.append(slabs[pl.ds(pl.multiple_of(at * slab, 8), slab), :])
        if rows % 2:
            planes.append(jnp.zeros_like(planes[0]))
        for g in range(pairs):
            left, right = planes[2 * g], pltpu.roll(planes[2 * g + 1], 64, 1)
            for j in range(COLS_IN_TILE):
                begin_lane = LAT * (j - 1)
                a, b = left, right
                if j == 0:
                    a = jnp.where(lane >= LANES - LAT, pltpu.roll(left, 1, 0), left)
                    b = jnp.where(
                        (lane >= 64 - LAT) & (lane < 64), pltpu.roll(right, 1, 0), right
                    )
                if j == COLS_IN_TILE - 1:
                    a = jnp.where(lane < LAT, pltpu.roll(left, slab - 1, 0), left)
                    b = jnp.where(
                        (lane >= 64) & (lane < 64 + LAT), pltpu.roll(right, slab - 1, 0), right
                    )
                low = begin_lane % LANES
                if low + 64 <= LANES:
                    inside = (lane >= low) & (lane < low + 64)
                else:
                    inside = (lane >= low) | (lane < low + 64 - LANES)
                mixed = pltpu.roll(jnp.where(inside, a, b), (-begin_lane) % LANES, 1)
                patches[
                    pl.ds((g * lat_frames + f) * padded + j, chunks, stride=COLS_IN_TILE), :
                ] = mixed[:chunks]

    low_patches = patches[...].astype(jnp.bfloat16)
    size = float(rows * columns * WIDTH)

    def front(g0, g1):
        stacked = jnp.concatenate(
            [
                low_patches[
                    (g * lat_frames + t + g0) * padded : (g * lat_frames + t + g1) * padded
                ]
                for t in range(3)
                for g in range(pairs)
            ],
            axis=1,
        )
        first[g0 * padded : g1 * padded] = jnp.dot(
            stacked, wide[...], preferred_element_type=jnp.float32
        )
        sums, squares = [], []
        for g in range(g0, g1):
            plain = square = jnp.zeros((8, C), jnp.float32)
            for r in range(rows):
                for top in range(g * padded, g * padded + columns, 8):
                    part = first[top : top + 8, r * C : (r + 1) * C]
                    plain = plain + part
                    square = square + part * part
            plain = jnp.sum(plain, axis=0, keepdims=True)
            square = jnp.sum(square, axis=0, keepdims=True)
            sums.append(plain)
            squares.append(square)
        n = g1 - g0
        fill = [jnp.zeros((1, C), jnp.float32)] * (-(2 * n) % 16)
        totals = group_sums(jnp.concatenate(sums + squares + fill, axis=0), matrix[...])
        mean = totals[:n] / size
        variance = totals[n : 2 * n] / size - mean * mean
        scale = lax.rsqrt(variance + EPSILON) * flat_terms[0:1]
        shift = flat_terms[1:2] - mean * scale
        for g in range(g0, g1):
            scale_g, shift_g = scale[g - g0 : g - g0 + 1], shift[g - g0 : g - g0 + 1]
            if g < 2:
                live = my_start - 2 + g >= 0
                scale_g, shift_g = jnp.where(live, scale_g, 0.0), jnp.where(live, shift_g, 0.0)
            for r in range(rows):
                part = first[g * padded : g * padded + columns, r * C : (r + 1) * C]
                act = half_silu(part * scale_g + shift_g)
                act = jnp.concatenate([act, jnp.zeros((stride - columns, C), jnp.float32)], axis=0)
                act = act.astype(jnp.bfloat16)
                acts[g * stride : (g + 1) * stride, r * C : (r + 1) * C] = act
                both = act if r == 0 else both + act
            if rows == 2:
                acts[g * stride : (g + 1) * stride, 2 * C :] = both

    kernel = [kernel_0.at[0], kernel_1.at[0], kernel_1.at[1]]
    inside = lax.broadcasted_iota(jnp.int32, (half, stride), 1) < columns
    group = 2 if frames % 2 == 0 else 1
    span = group * stride

    def terms(y, place):
        return [(y, place, t, c) for t in range(3) for c in range(C // LANES)]

    def product(f0, parts):
        weights = jnp.concatenate(
            [kernel[t][y][:, c * LANES : (c + 1) * LANES] for y, _, t, c in parts], axis=1
        )
        positions = jnp.concatenate(
            [
                acts[
                    (f0 + t) * stride : (f0 + t) * stride + span,
                    p * C + c * LANES : p * C + (c + 1) * LANES,
                ]
                for _, p, t, c in parts
            ],
            axis=1,
        )
        return lax.dot_general(
            weights, positions, (((1,), (1,)), ((), ())), preferred_element_type=jnp.float32
        )

    def back(f0):
        if rows == 2:
            middle = terms(1, 2)
            keep = len(middle) // 2 * 2
            shared = product(f0, middle[:keep])
            taps = [
                shared + product(f0, terms(2, 1) + middle[keep:]),
                shared + product(f0, terms(0, 0) + middle[keep:]),
            ]
        else:
            taps = []
            for r in range(rows):
                places = range(max(0, r - 1), min(rows - 1, r + 1) + 1)
                taps.append(product(f0, [q for p in places for q in terms(p - r + 1, p)]))
        band = lax.axis_index("band")
        for i in range(group):
            plain = square = jnp.zeros((half, stride), jnp.float32)
            own = [jnp.zeros((half, stride), jnp.float32)] * own_rows
            for r in range(rows):
                tap = [
                    taps[r][s * half : (s + 1) * half, i * stride : (i + 1) * stride]
                    for s in range(3)
                ]
                value = tap[1] + pltpu.roll(tap[0], 1, 1) + pltpu.roll(tap[2], stride - 1, 1)
                value = jnp.where(inside, value, 0.0)
                plain = plain + value
                square = square + value * value
                own = [
                    value if r == 0 else jnp.where(band * own_rows + inner == r, value, own[inner])
                    for inner in range(own_rows)
                ]
            mean = group_columns(plain, size)
            power = group_columns(square, size)
            inverse = [lax.rsqrt(p - m * m + EPSILON) for p, m in zip(power, mean)]
            scale = group_rows(inverse, half, stride) * tall_terms[0]
            shift = tall_terms[1] - group_rows(mean, half, stride) * scale
            for inner in range(own_rows):
                value = half_silu(own[inner] * scale + shift)
                value = jnp.where(f0 + i < my_count, value, 0.0).astype(out.dtype)
                out[f0 + i, inner] = value[:, :columns]

    front(0, frames + 2)
    for f0 in range(0, frames, group):
        back(f0)


def shards(latents, frame_counts, w_in, gain_in, shift_in, w_mid, gain_out, shift_out):
    frames, own_rows, flat = latents.shape
    columns = flat // LAT
    half = w_mid.shape[4]
    blocks, bands = lax.axis_size("block"), lax.axis_size("band")
    rows = own_rows * bands
    use_ring = small_slice(blocks, bands, own_rows, lax.axis_size("chan"))
    own = jnp.transpose(latents, (1, 0, 2))
    middle = jnp.transpose(w_mid, (0, 1, 2, 4, 3)).reshape(3, 3, 3 * half, C)
    kept, *prepared = prepare(
        (blocks, rows, own_rows, frames, use_ring),
        own,
        w_in,
        gain_in,
        shift_in,
        gain_out,
        shift_out,
        frame_counts,
        middle,
    )
    prepared.append(load_rest(rows, middle))
    if use_ring:
        sources = exchange_ring(own, kept)
    else:
        gathered = lax.all_gather(kept, ("block", "band"), axis=0)
        sources = [gathered.reshape(-1, frames, flat)]
    pieces = tuple(a.shape[0] for a in sources)
    chunks = columns // COLS_IN_TILE
    slab = -(-(chunks + 1) // 8) * 8
    padded = -(-(columns + 1) // 16) * 16
    stride = -(-(columns + 1) // LANES) * LANES
    pairs = -(-rows // 2)
    cfg = (rows, frames, columns, pieces)
    vmem = pl.BlockSpec(memory_space=pltpu.VMEM)
    decoded = pl.pallas_call(
        functools.partial(body, cfg),
        out_shape=jax.ShapeDtypeStruct((frames, own_rows, half, columns), jnp.bfloat16),
        in_specs=[vmem] * (len(sources) + len(prepared)),
        out_specs=vmem,
        scratch_shapes=[
            pltpu.VMEM((sum(pieces) * frames * slab, LANES), jnp.float32),
            pltpu.VMEM((pairs * (frames + HALO) * padded, LANES), jnp.float32),
            pltpu.VMEM(((frames + 2) * padded, rows * C), jnp.float32),
            pltpu.VMEM(((frames + 2) * stride, (rows + (rows == 2)) * C), jnp.bfloat16),
        ],
        compiler_params=pltpu.CompilerParams(vmem_limit_bytes=32 * 1024 * 1024),
    )(*sources, *prepared)
    return jnp.transpose(decoded, (0, 1, 3, 2))


def small_slice(blocks, bands, own_rows, cores):
    return blocks == 4 and bands == 2 and own_rows == 1 and cores == 2


def solution(mesh):
    return jax.shard_map(
        shards,
        mesh=mesh,
        in_specs=(
            P(("video", "block"), "band", None),
            P("video"),
            P(),
            P(),
            P(),
            P(None, None, None, None, "chan"),
            P("chan"),
            P("chan"),
        ),
        out_specs=P(("video", "block"), "band", None, "chan"),
        check_vma=False,
    )
```
